256 devices in a mesh: shard: 16 (over z, core), tensor: 4 (over x), section: 4 (over y).
Axes of the slice: x: 4, y: 4, z: 8, core: 2. Of those that a mesh axis runs over, the one named last changes fastest.
Arguments:
- gradient: bfloat16 [6, 2048, 8192], P(None, ('tensor', 'section'), 'shard'), may hold values from -6 to 6
- basis: bfloat16 [6, 2048, 256], P(None, ('tensor', 'section')), may hold values from -6 to 6
- moment_m: float32 [6, 8192, 256], P(None, ('shard', 'tensor', 'section')), may hold values from -4 to 4
- moment_v: float32 [6, 8192, 256], P(None, ('shard', 'tensor', 'section')), may hold values from 0.002 to 0.02
Outputs:
- delta: bfloat16 [6, 2048, 8192], P(None, ('tensor', 'section'), 'shard')
- basis_new: bfloat16 [6, 2048, 256], P(None, ('tensor', 'section'))
- moment_m_new: float32 [6, 8192, 256], P(None, ('shard', 'tensor', 'section'))
- moment_v_new: float32 [6, 8192, 256], P(None, ('shard', 'tensor', 'section'))
The draws below stay inside these ranges and needn't reach their ends.
All inputs are finite; a program needn't handle non-finite values. Where the reference program divides by a largest or mean magnitude, that divisor is 1e-20 or more.
Results may differ from the reference program's by a relative error of at most 0.0049.
Values may be sent and summed in bfloat16 or wider, within the bound.
A program may use at most 64 MiB of HBM per device.

```python
import math
import jax
import jax.numpy as jnp
from jax import lax

D = 2048
FF = 8192
RANK = 256
NS_ITERS = 4
NMAT = 6


def raised(result, rng, source, target, parts, factor):
    owner, partner = [(jnp.arange(result.shape[dim]) // (result.shape[dim] // parts)).reshape([-1 if axis == dim else 1 for axis in range(result.ndim)]) for dim in (source, target)]
    chosen = jax.random.permutation(rng, parts)[partner]
    strong = (owner == chosen) | (owner == (partner + parts // 2) % parts)
    return jnp.where(strong, factor * result, result)


def levels(key, shape, shards, least, high):
    def one(axis_at, blocks):
        steps = jax.random.uniform(jax.random.fold_in(jax.random.fold_in(key, 6), axis_at), (blocks,), jnp.float32, least / len(shards), high / len(shards))
        return jnp.repeat(jnp.exp(steps), shape[axis_at] // blocks).reshape((-1,) + (1,) * (len(shape) - axis_at - 1))

    level = one(*shards[0])
    for cut in shards[1:]:
        level = level * one(*cut)
    return level


def bell_draw(rng, dims, deviation, reach, split=(), kind=jnp.bfloat16):
    values = deviation * jax.random.normal(rng, dims, jnp.float32)
    if split:
        values = values * levels(rng, dims, split, -0.22, 0.18)
    return jnp.clip(values, -reach, reach).astype(kind)


def noise_with(rng, dims, spread, bound, pieces, heavy, kind=jnp.bfloat16):
    drawn = spread * jax.random.normal(rng, dims, jnp.float32)
    if pieces:
        drawn = drawn * levels(rng, dims, pieces, -0.22, 0.18)
    return jnp.clip(raised(drawn, jax.random.fold_in(rng, 3), *heavy), -bound, bound).astype(kind)


def setup_inputs(seed: int = 0) -> dict:
    arg_keys = jax.random.split(jax.random.key(seed), 5)
    gradient = noise_with(arg_keys[0], (NMAT, D, FF), 1.0, 6.0, ((1, 16), (2, 16)), (1, 2, 16, 2.0))
    basis = bell_draw(arg_keys[1], (NMAT, D, RANK), 1.0, 6.0, ((1, 16),))
    moment_m = bell_draw(arg_keys[2], (NMAT, FF, RANK), 0.5, 4.0, ((1, 256),), jnp.float32)
    moment_v = jnp.clip(jnp.exp(math.log(0.02) - 2.30258502 * jax.random.uniform(arg_keys[3], (NMAT, FF, RANK), jnp.float32) ** levels(arg_keys[3], (NMAT, FF, RANK), ((1, 256),), -0.2, 0.2)), 0.002, 0.02)
    return dict(gradient=gradient, basis=basis, moment_m=moment_m, moment_v=moment_v)


beta_one = 0.9
beta_two = 0.999
bias_one = 1.0 - 0.9 ** 10
bias_two = 1.0 - 0.999 ** 10
eps_adam = 1e-08
galore_gain = 4.0

def reference(gradient, basis, moment_m, moment_v):
    width_root = math.sqrt(D)
    grad_float = gradient.astype(jnp.float32)
    basis_float = basis.astype(jnp.float32)
    low_rank = jnp.einsum('kmn,kmr->knr', grad_float, basis_float) / width_root
    moment_m_new = beta_one * moment_m + (1.0 - beta_one) * low_rank
    moment_v_new = beta_two * moment_v + (1.0 - beta_two) * low_rank * low_rank
    step_low = (moment_m_new / bias_one / (jnp.sqrt(moment_v_new / bias_two) + eps_adam)).astype(jnp.bfloat16)
    delta = (-galore_gain / width_root * jnp.einsum('kmr,knr->kmn', basis_float, step_low.astype(jnp.float32))).astype(jnp.bfloat16)
    rough_low = low_rank.astype(jnp.bfloat16)
    subspace = jnp.einsum('kmn,knr->kmr', grad_float, rough_low.astype(jnp.float32))
    gram_mat = jnp.einsum('kmr,kms->krs', subspace, subspace, precision=lax.Precision.HIGHEST)
    row_bound = lax.optimization_barrier(jnp.max(lax.optimization_barrier(jnp.sum(jnp.abs(gram_mat), axis=2)), axis=1))[:, None, None] + 1e-06
    iterate = subspace / jnp.sqrt(row_bound)
    gram_mat = gram_mat / row_bound
    identity = jnp.eye(RANK, dtype=jnp.float32)
    for turn_index in range(NS_ITERS):
        factor = 1.5 * identity - 0.5 * gram_mat
        iterate = jnp.einsum('kmr,krs->kms', iterate, factor, precision=lax.Precision.HIGHEST)
        gram_mat = jnp.einsum('kmr,kms->krs', iterate, iterate, precision=lax.Precision.HIGHEST)
    basis_new = (width_root * iterate).astype(jnp.bfloat16)
    return (delta, basis_new, moment_m_new, moment_v_new)
```

```python
import functools
import math

import jax
import jax.numpy as jnp
from jax import lax
from jax.experimental import pallas as pl
from jax.experimental.pallas import tpu as pltpu
from jax.sharding import PartitionSpec as P

D = 2048
NS_ITERS = 4
NMAT = 6
RANK = 256
ROWS = 128
RING = 4
PART = 32
ORDER = (0, 3, 1, 4, 2, 5)

beta_one = 0.9
beta_two = 0.999
bias_one = 1.0 - 0.9**10
bias_two = 1.0 - 0.999**10
eps_adam = 1e-08
galore_gain = 4.0

F32 = jnp.float32
BF16 = jnp.bfloat16
MESH = pl.DeviceIdType.MESH


def dot(a, b, ca, cb):
    return lax.dot_general(a, b, (((ca,), (cb,)), ((), ())), preferred_element_type=F32)


def split(a):
    high = a.astype(BF16)
    return high, (a - high.astype(F32)).astype(BF16)


def dot3(a, b, ca=1, cb=0):
    (ah, al), (bh, bl) = a, b
    return dot(ah, bh, ca, cb) + (dot(ah, bl, ca, cb) + dot(al, bh, ca, cb))


def kernel(
    depth,
    g_hbm,
    b_hbm,
    m_hbm,
    v_hbm,
    delta_hbm,
    basis_hbm,
    m_out_hbm,
    v_out_hbm,
    g_v,
    b_v,
    m_v,
    v_v,
    p_f,
    p_b,
    r1,
    rel1,
    q_f,
    q_b,
    r2,
    rel2,
    rough,
    step,
    t_own,
    t_in,
    u_b,
    d_in,
    s_f,
    gram,
    gram_in,
    gram_all,
    base,
    del_v,
    load_sem,
    store_sem,
    rs_send,
    rs_recv,
    ag_send,
    ag_recv,
    t_send,
    t_recv,
    d_send,
    d_recv,
    gr_send,
    gr_recv,
    ga_send,
    ga_recv,
    f_send,
    f_recv,
    fc_send,
    fc_recv,
):
    shard = lax.axis_index("shard")
    x = lax.axis_index("tensor")
    y = lax.axis_index("section")
    z, core = shard // 2, lax.rem(shard, 2)
    partner = {"shard": z * 2 + (1 - core)}
    places = {"tensor": x, "section": y}

    loads = []
    for k in ORDER:
        pair = (
            pltpu.make_async_copy(g_hbm.at[k], g_v.at[k], load_sem.at[0, k]),
            pltpu.make_async_copy(b_hbm.at[k], b_v.at[k], load_sem.at[1, k]),
        )
        for copy in pair:
            copy.start()
        loads.append(pair)
    moments = (
        pltpu.make_async_copy(m_hbm, m_v, load_sem.at[2, 0]),
        pltpu.make_async_copy(v_hbm, v_v, load_sem.at[2, 1]),
    )
    for copy in moments:
        copy.start()

    barrier = pltpu.get_barrier_semaphore()
    greeted = 0
    for dx in range(RING):
        for dy in range(RING):
            if dx or dy:
                there = {"tensor": lax.rem(x + dx, RING), "section": lax.rem(y + dy, RING)}
                pl.semaphore_signal(barrier, inc=1, device_id=there, device_id_type=MESH)
                greeted += 1
    for dz in range(1, depth):
        there = {"shard": lax.rem(z + dz, depth) * 2 + core}
        pl.semaphore_signal(barrier, inc=1, device_id=there, device_id_type=MESH)
        greeted += 1
    pl.semaphore_signal(barrier, inc=1, device_id=partner, device_id_type=MESH)
    greeted += 1

    def project(k):
        g_copy, b_copy = loads[ORDER.index(k)]
        g_copy.wait()
        b_copy.wait()
        part = dot(g_v[k], b_v[k], 0, 0).reshape(RING, RING, PART, RANK)
        p_f[k] = part
        p_b[k] = part.astype(BF16)

    project(ORDER[0])
    pl.semaphore_wait(barrier, greeted)

    sends = []

    def push(src, dst, send_sem, recv_sem, where):
        copy = pltpu.make_async_remote_copy(
            src_ref=src,
            dst_ref=dst,
            send_sem=send_sem,
            recv_sem=recv_sem,
            device_id=where,
            device_id_type=MESH,
        )
        copy.start()
        return copy

    def ring_of(k, stage):
        name = ("tensor", "section")[(stage + (k >= 3)) % 2]
        at = places[name]
        plus, minus, far = (lax.rem(at + i, RING) for i in (1, 3, 2))
        return name, at, plus, minus, far

    def half(h, size):
        return pl.ds(h * size, size)

    def rs_piece(source, k, stage, at, h):
        if stage == 1:
            return source.at[k, at, half(h, PART // 2)]
        if k < 3:
            return source.at[k, at, half(h, 2)]
        return source.at[k, half(h, 2), at]

    def rs_parts(stage):
        return ((p_f, p_b, r1, rel1), (q_f, q_b, r2, rel2))[stage]

    def rs_push(k, stage, src, slot, to):
        name = ring_of(k, stage)[0]
        landing = rs_parts(stage)[2]
        return push(
            src, landing.at[k, slot], rs_send.at[stage, k, slot], rs_recv.at[stage, k, slot], {name: to}
        )

    def rs_start(k, stage):
        name, at, plus, minus, far = ring_of(k, stage)
        source = rs_parts(stage)[1]
        copies = {}
        for slot, to_at, h, to in ((0, far, 0, plus), (1, far, 1, minus), (2, plus, 1, plus), (3, minus, 0, minus)):
            copies[slot] = rs_push(k, stage, rs_piece(source, k, stage, to_at, h), slot, to)
        sends.extend(copies.values())
        return copies

    def rs_relay(k, stage, copies):
        name, at, plus, minus, far = ring_of(k, stage)
        exact, _, landing, relay = rs_parts(stage)
        for slot, h, to in ((0, 0, plus), (1, 1, minus)):
            copies[slot].wait_recv()
            own = rs_piece(exact, k, stage, to, h)[...]
            relay[k, slot] = (own + landing[k, slot].astype(F32)).astype(BF16)
            copies[slot + 4] = rs_push(k, stage, relay.at[k, slot], slot + 4, to)
            sends.append(copies[slot + 4])

    def rs_finish(k, stage, copies):
        name, at, plus, minus, far = ring_of(k, stage)
        exact, _, landing, _ = rs_parts(stage)
        totals = []
        for h, slots in ((0, (3, 4)), (1, (2, 5))):
            total = rs_piece(exact, k, stage, at, h)[...]
            for slot in slots:
                copies[slot].wait_recv()
                total = total + landing[k, slot].astype(F32)
            totals.append(total)
        return totals

    flight = {ORDER[0]: rs_start(ORDER[0], 0)}
    for k in ORDER[1:]:
        project(k)
        flight[k] = rs_start(k, 0)
    for k in ORDER:
        rs_relay(k, 0, flight[k])
    later = {}
    for k in ORDER:
        for h, total in enumerate(rs_finish(k, 0, flight[k])):
            q_f[k, 2 * h : 2 * h + 2] = total
            q_b[k, 2 * h : 2 * h + 2] = total.astype(BF16)
        later[k] = rs_start(k, 1)
    for k in ORDER:
        rs_relay(k, 1, later[k])

    def ag_piece(held, k, stage, at, h):
        if stage == 0:
            if k < 3:
                return held.at[k, x, at, half(h, PART // 2)]
            return held.at[k, at, y, half(h, PART // 2)]
        if k < 3:
            return held.at[k, at, half(h, 2)]
        return held.at[k, half(h, 2), at]

    def ag_push(held, kind, k, stage, at, h, slot, to):
        name = ring_of(k, 1 - stage)[0]
        piece = ag_piece(held, k, stage, at, h)
        copy = push(piece, piece, ag_send.at[kind, stage, k, slot], ag_recv.at[kind, stage, k, slot], {name: to})
        sends.append(copy)
        return copy

    def ag_start(held, kind, k, stage):
        name, at, plus, minus, far = ring_of(k, 1 - stage)
        return {
            slot: ag_push(held, kind, k, stage, at, h, slot, to)
            for slot, h, to in ((0, 0, plus), (3, 1, minus), (1, 1, plus), (2, 0, minus))
        }

    def ag_relay(held, kind, k, stage, copies):
        name, at, plus, minus, far = ring_of(k, 1 - stage)
        copies[0].wait_recv()
        copies[4] = ag_push(held, kind, k, stage, minus, 0, 4, plus)
        copies[3].wait_recv()
        copies[5] = ag_push(held, kind, k, stage, plus, 1, 5, minus)

    def ag_finish(copies):
        for slot in (1, 2, 4, 5):
            copies[slot].wait_recv()

    for copy in moments:
        copy.wait()
    stores = []

    def store(src, dst, sem):
        copy = pltpu.make_async_copy(src, dst, sem)
        copy.start()
        stores.append(copy)

    gather = {}
    for k in ORDER:
        low = jnp.concatenate(rs_finish(k, 1, later[k]), axis=0) * (1.0 / math.sqrt(D))
        rough[k, x, y] = low.astype(BF16)
        gather[k] = ag_start(rough, 0, k, 0)
        first = beta_one * m_v[k] + (1.0 - beta_one) * low
        second = beta_two * v_v[k] + (1.0 - beta_two) * low * low
        m_v[k] = first
        v_v[k] = second
        step[k, x, y] = (first / bias_one / (jnp.sqrt(second / bias_two) + eps_adam)).astype(BF16)
    store(m_v, m_out_hbm, store_sem.at[2, 0])
    store(v_v, v_out_hbm, store_sem.at[2, 1])

    for k in ORDER:
        ag_relay(rough, 0, k, 0, gather[k])
    wide = {}
    for k in ORDER:
        ag_finish(gather[k])
        wide[k] = ag_start(rough, 0, k, 1)
    for k in ORDER:
        ag_relay(rough, 0, k, 1, wide[k])
    walk = {k: ag_start(step, 1, k, 0) for k in ORDER}

    def core_copy(k):
        return pltpu.make_async_remote_copy(
            src_ref=t_own.at[k],
            dst_ref=t_in.at[k],
            send_sem=t_send.at[k],
            recv_sem=t_recv.at[k],
            device_id=partner,
            device_id_type=MESH,
        )

    for k in ORDER:
        ag_finish(wide[k])
        t_own[k] = dot(g_v[k], rough[k].reshape(RING * RING * PART, RANK), 1, 0)

        @pl.when(core != k % 2)
        def _():
            core_copy(k).start()

    for k in ORDER:
        ag_relay(step, 1, k, 0, walk[k])

    def plane_copy(k):
        return pltpu.make_async_remote_copy(
            src_ref=u_b.at[k],
            dst_ref=d_in.at[z],
            send_sem=d_send.at[k],
            recv_sem=d_recv.at[z],
            device_id={"shard": 2 * k + k % 2},
            device_id_type=MESH,
        )

    for k in ORDER:

        @pl.when(core == k % 2)
        def _():
            core_copy(k).wait_recv()
            both = t_own[k] + t_in[k]

            @pl.when(z == k)
            def _():
                s_f[...] = both

            @pl.when(z != k)
            def _():
                u_b[k] = both.astype(BF16)
                plane_copy(k).start()

    stride = {}
    for k in ORDER:
        ag_finish(walk[k])
        stride[k] = ag_start(step, 1, k, 1)
    for k in ORDER:
        ag_relay(step, 1, k, 1, stride[k])

    def delta(k):
        ag_finish(stride[k])
        product = dot(b_v[k], step[k].reshape(RING * RING * PART, RANK), 1, 1)
        del_v[k] = (-galore_gain / math.sqrt(D) * product).astype(BF16)
        store(del_v.at[k], delta_hbm.at[k], store_sem.at[0, k])

    owner = jnp.logical_and(z < NMAT, core == lax.rem(z, 2))
    chunk = RANK // (RING * RING)
    mine = pl.ds(pl.multiple_of((x * RING + y) * chunk, chunk), chunk)
    others = [(dx, dy) for dx in (2, 1, 3, 0) for dy in (2, 1, 3, 0) if dx or dy]

    def gram_copy(dx, dy):
        tx, ty = lax.rem(x + dx, RING), lax.rem(y + dy, RING)
        slot = dx * RING + dy
        return pltpu.make_async_remote_copy(
            src_ref=gram.at[pl.ds(pl.multiple_of((tx * RING + ty) * chunk, chunk), chunk)],
            dst_ref=gram_in.at[slot],
            send_sem=gr_send.at[slot],
            recv_sem=gr_recv.at[slot],
            device_id={"tensor": tx, "section": ty},
            device_id_type=MESH,
        )

    def gram_spread(dx, dy):
        slot = dx * RING + dy
        return pltpu.make_async_remote_copy(
            src_ref=gram_all.at[mine],
            dst_ref=gram_all.at[mine],
            send_sem=ga_send.at[slot],
            recv_sem=ga_recv.at[slot],
            device_id={"tensor": lax.rem(x + dx, RING), "section": lax.rem(y + dy, RING)},
            device_id_type=MESH,
        )

    @pl.when(owner)
    def _():
        for source in range(depth):

            @pl.when(z != source)
            def _():
                pltpu.make_async_remote_copy(
                    src_ref=u_b.at[0],
                    dst_ref=d_in.at[source],
                    send_sem=d_send.at[0],
                    recv_sem=d_recv.at[source],
                    device_id=partner,
                    device_id_type=MESH,
                ).wait_recv()
                s_f[...] += d_in[source].astype(F32)

        whole = split(s_f[...])
        gram[...] = dot3(whole, whole, 0, 0)
        for dx, dy in others:
            gram_copy(dx, dy).start()

    for k in ORDER[:3]:
        delta(k)

    @pl.when(owner)
    def _():
        total = gram[mine]
        for dx, dy in others:
            gram_copy(dx, dy).wait_recv()
            total = total + gram_in[dx * RING + dy]
        gram_all[mine] = total
        for dx, dy in others:
            gram_spread(dx, dy).start()

    for k in ORDER[3:]:
        delta(k)

    def basis_copy(dz):
        return pltpu.make_async_remote_copy(
            src_ref=base.at[z],
            dst_ref=base.at[z],
            send_sem=f_send.at[dz],
            recv_sem=f_recv.at[z],
            device_id={"shard": lax.rem(z + dz, depth) * 2 + core},
            device_id_type=MESH,
        )

    def basis_cross(k):
        return pltpu.make_async_remote_copy(
            src_ref=base.at[k],
            dst_ref=base.at[k],
            send_sem=fc_send.at[k],
            recv_sem=fc_recv.at[k],
            device_id=partner,
            device_id_type=MESH,
        )

    @pl.when(owner)
    def _():
        for dx, dy in others:
            gram_spread(dx, dy).wait_recv()
        gram0 = gram_all[...]
        row_sum = jnp.sum(jnp.abs(gram0), axis=1, keepdims=True)
        bound = jnp.max(row_sum, axis=0, keepdims=True) + 1e-06
        iterate = s_f[...] / jnp.sqrt(bound)
        gram_mat = gram0 / bound
        line = lax.broadcasted_iota(jnp.int32, (RANK, RANK), 0)
        column = lax.broadcasted_iota(jnp.int32, (RANK, RANK), 1)
        identity = jnp.where(line == column, 1.5, 0.0).astype(F32)
        for turn in range(NS_ITERS):
            factor = split(identity - 0.5 * gram_mat)
            if turn + 1 < NS_ITERS:
                gram_mat = dot3(split(dot3(split(gram_mat), factor)), factor)
            iterate = dot3(split(iterate), factor)
        base[z] = (math.sqrt(D) * iterate).astype(BF16)
        for dz in (4, 3, 5, 2, 6, 1, 7):
            basis_copy(dz).start()

    for k in range(NMAT):

        @pl.when(core == k % 2)
        def _():
            @pl.when(z != k)
            def _():
                pltpu.make_async_remote_copy(
                    src_ref=base.at[k],
                    dst_ref=base.at[k],
                    send_sem=f_send.at[0],
                    recv_sem=f_recv.at[k],
                    device_id=partner,
                    device_id_type=MESH,
                ).wait_recv()

            basis_cross(k).start()

    for k in range(NMAT):

        @pl.when(core != k % 2)
        def _():
            basis_cross(k).wait_recv()

        store(base.at[k], basis_hbm.at[k], store_sem.at[1, k])

    for copy in sends:
        copy.wait_send()
    for k in range(NMAT):

        @pl.when(core != k % 2)
        def _():
            core_copy(k).wait_send()

        @pl.when(core == k % 2)
        def _():
            basis_cross(k).wait_send()

            @pl.when(z != k)
            def _():
                plane_copy(k).wait_send()

    @pl.when(owner)
    def _():
        for dx, dy in others:
            gram_copy(dx, dy).wait_send()
            gram_spread(dx, dy).wait_send()
        for dz in range(1, depth):
            basis_copy(dz).wait_send()

    for copy in stores:
        copy.wait()


def per_device(depth, gradient, basis, moment_m, moment_v):
    dma = pltpu.SemaphoreType.DMA
    anywhere = pl.BlockSpec(memory_space=pl.ANY)
    shape = jax.ShapeDtypeStruct
    scratch = [
        pltpu.VMEM(gradient.shape, BF16),
        pltpu.VMEM(basis.shape, BF16),
        pltpu.VMEM(moment_m.shape, F32),
        pltpu.VMEM(moment_v.shape, F32),
        pltpu.VMEM((NMAT, RING, RING, PART, RANK), F32),
        pltpu.VMEM((NMAT, RING, RING, PART, RANK), BF16),
        pltpu.VMEM((NMAT, 6, 2, PART, RANK), BF16),
        pltpu.VMEM((NMAT, 2, 2, PART, RANK), BF16),
        pltpu.VMEM((NMAT, RING, PART, RANK), F32),
        pltpu.VMEM((NMAT, RING, PART, RANK), BF16),
        pltpu.VMEM((NMAT, 6, PART // 2, RANK), BF16),
        pltpu.VMEM((NMAT, 2, PART // 2, RANK), BF16),
        pltpu.VMEM((NMAT, RING, RING, PART, RANK), BF16),
        pltpu.VMEM((NMAT, RING, RING, PART, RANK), BF16),
        pltpu.VMEM((NMAT, ROWS, RANK), F32),
        pltpu.VMEM((NMAT, ROWS, RANK), F32),
        pltpu.VMEM((NMAT, ROWS, RANK), BF16),
        pltpu.VMEM((depth, ROWS, RANK), BF16),
        pltpu.VMEM((ROWS, RANK), F32),
        pltpu.VMEM((RANK, RANK), F32),
        pltpu.VMEM((RING * RING, RANK // (RING * RING), RANK), F32),
        pltpu.VMEM((RANK, RANK), F32),
        pltpu.VMEM((NMAT, ROWS, RANK), BF16),
        pltpu.VMEM(gradient.shape, BF16),
        dma((3, NMAT)),
        dma((3, NMAT)),
        dma((2, NMAT, 6)),
        dma((2, NMAT, 6)),
        dma((2, 2, NMAT, 6)),
        dma((2, 2, NMAT, 6)),
        dma((NMAT,)),
        dma((NMAT,)),
        dma((NMAT,)),
        dma((depth,)),
        dma((RING * RING,)),
        dma((RING * RING,)),
        dma((RING * RING,)),
        dma((RING * RING,)),
        dma((depth,)),
        dma((NMAT,)),
        dma((NMAT,)),
        dma((NMAT,)),
    ]
    return pl.pallas_call(
        functools.partial(kernel, depth),
        out_shape=(
            shape(gradient.shape, BF16),
            shape(basis.shape, BF16),
            shape(moment_m.shape, F32),
            shape(moment_v.shape, F32),
        ),
        in_specs=[anywhere] * 4,
        out_specs=(anywhere,) * 4,
        scratch_shapes=scratch,
        compiler_params=pltpu.CompilerParams(
            collective_id=0, has_side_effects=True, vmem_limit_bytes=48 * 1024 * 1024
        ),
        name="galore_step",
    )(gradient, basis, moment_m, moment_v)


def solution(mesh):
    placed = (
        P(None, ("tensor", "section"), "shard"),
        P(None, ("tensor", "section"), None),
        P(None, ("shard", "tensor", "section"), None),
        P(None, ("shard", "tensor", "section"), None),
    )
    return jax.shard_map(
        functools.partial(per_device, mesh.shape["shard"] // 2),
        mesh=mesh,
        in_specs=placed,
        out_specs=placed,
        check_vma=False,
    )
```

```python
import functools
import math

import jax
import jax.numpy as jnp
from jax import lax
from jax.experimental import pallas as pl
from jax.experimental.pallas import tpu as pltpu
from jax.sharding import PartitionSpec as P

D = 2048
NS_ITERS = 4
NMAT = 6
RANK = 256
ROWS = 128
RING = 4
PART = 32
SETS = ((0, 3), (1, 4), (2, 5))
LAG = 1

beta_one = 0.9
beta_two = 0.999
bias_one = 1.0 - 0.9**10
bias_two = 1.0 - 0.999**10
eps_adam = 1e-08
galore_gain = 4.0

F32 = jnp.float32
BF16 = jnp.bfloat16
MESH = pl.DeviceIdType.MESH


def dot(a, b, ca, cb):
    return lax.dot_general(a, b, (((ca,), (cb,)), ((), ())), preferred_element_type=F32)


def split(a):
    high = a.astype(BF16)
    return high, (a - high.astype(F32)).astype(BF16)


def dot3(a, b, ca=1, cb=0):
    (ah, al), (bh, bl) = a, b
    return dot(ah, bh, ca, cb) + (dot(ah, bl, ca, cb) + dot(al, bh, ca, cb))


def kernel(
    depth,
    g_hbm,
    b_hbm,
    m_hbm,
    v_hbm,
    delta_out,
    basis_out,
    m_out,
    v_out,
    g_v,
    b_v,
    m_v,
    v_v,
    p_f,
    p_b,
    r1,
    rel1,
    q_f,
    q_b,
    r2,
    rel2,
    rough,
    step,
    t_own,
    t_in,
    u_b,
    d_in,
    s_f,
    gram,
    gram_in,
    gram_all,
    base,
    del_v,
    load_sem,
    store_sem,
    ring_send,
    rs_recv,
    ag_recv,
    t_recv,
    f_recv,
    fc_recv,
    one_sem,
):
    t_send, d_send, d_recv, gr_send, gr_recv, ga_send, ga_recv, f_send, fc_send = (one_sem.at[i] for i in range(9))
    shard = lax.axis_index("shard")
    x = lax.axis_index("tensor")
    y = lax.axis_index("section")
    z, core = shard // 2, lax.rem(shard, 2)
    partner = {"shard": z * 2 + (1 - core)}
    places = {"tensor": x, "section": y}
    owner = jnp.logical_and(z < NMAT, core == lax.rem(z, 2))

    def local(src, dst, sem):
        copy = pltpu.make_async_copy(src, dst, sem)
        copy.start()
        return copy

    def remote(src, dst, send_sem, recv_sem, where):
        return pltpu.make_async_remote_copy(
            src_ref=src,
            dst_ref=dst,
            send_sem=send_sem,
            recv_sem=recv_sem,
            device_id=where,
            device_id_type=MESH,
        )

    def arrived(like, sem):
        remote(like, like, sem, sem, partner).wait_recv()

    def departed(like, sem):
        remote(like, like, sem, sem, partner).wait_send()

    barrier = pltpu.get_barrier_semaphore()
    peers = [
        {"tensor": lax.rem(x + dx, RING), "section": lax.rem(y + dy, RING)}
        for dx in range(RING)
        for dy in range(RING)
        if dx or dy
    ]
    peers += [{"shard": lax.rem(z + dz, depth) * 2 + core} for dz in range(1, depth)]
    peers.append(partner)
    for there in peers:
        pl.semaphore_signal(barrier, inc=1, device_id=there, device_id_type=MESH)

    b_load = local(b_hbm, b_v, load_sem.at[NMAT])
    g_load = {k: local(g_hbm.at[k], g_v.at[k], load_sem.at[k]) for group in SETS for k in group}
    m_load = local(m_hbm, m_v, load_sem.at[NMAT + 1])
    v_load = local(v_hbm, v_v, load_sem.at[NMAT + 2])

    def project(k):
        g_load[k].wait()
        part = dot(g_v[k], b_v[k], 0, 0).reshape(RING, RING, PART, RANK)
        p_f[k] = part
        p_b[k] = part.astype(BF16)

    b_load.wait()
    for k in SETS[0]:
        project(k)
    pl.semaphore_wait(barrier, len(peers))

    def ring_of(k, stage):
        name = ("tensor", "section")[(stage + (k >= 3)) % 2]
        at = places[name]
        plus, minus, far = (lax.rem(at + i, RING) for i in (1, 3, 2))
        return name, at, plus, minus, far

    def half(h, size):
        return pl.ds(h * size, size)

    def rs_piece(source, k, stage, at, h):
        if stage == 1:
            return source.at[k, at, half(h, PART // 2)]
        if k < 3:
            return source.at[k, at, half(h, 2)]
        return source.at[k, half(h, 2), at]

    rs_parts = ((p_f, p_b, r1, rel1), (q_f, q_b, r2, rel2))

    def rs_push(k, stage, src, slot, to):
        sem = rs_recv.at[stage, k % 3, int(slot >= 2)]
        remote(src, rs_parts[stage][2].at[k, slot], ring_send.at[stage], sem, {ring_of(k, stage)[0]: to}).start()

    def rs_start(group, stage):
        source = rs_parts[stage][1]
        for first in (True, False):
            for k in group:
                name, at, plus, minus, far = ring_of(k, stage)
                if first:
                    rs_push(k, stage, rs_piece(source, k, stage, far, 0), 0, plus)
                    rs_push(k, stage, rs_piece(source, k, stage, far, 1), 1, minus)
                else:
                    rs_push(k, stage, rs_piece(source, k, stage, plus, 1), 2, plus)
                    rs_push(k, stage, rs_piece(source, k, stage, minus, 0), 3, minus)

    def rs_relay(group, stage):
        exact, _, landing, relay = rs_parts[stage]
        arrived(landing.at[0, pl.ds(0, 4)], rs_recv.at[stage, group[0] % 3, 0])
        for k in group:
            name, at, plus, minus, far = ring_of(k, stage)
            for slot, to in ((0, plus), (1, minus)):
                own = rs_piece(exact, k, stage, to, slot)[...]
                relay[k, slot] = (own + landing[k, slot].astype(F32)).astype(BF16)
                rs_push(k, stage, relay.at[k, slot], slot + 4, to)

    def rs_finish(group, stage):
        exact, _, landing, _ = rs_parts[stage]
        arrived(landing.at[pl.ds(0, 2), pl.ds(0, 4)], rs_recv.at[stage, group[0] % 3, 1])
        totals = {}
        for k in group:
            at = ring_of(k, stage)[1]
            for h, (one, two) in enumerate(((3, 4), (2, 5))):
                own = rs_piece(exact, k, stage, at, h)[...]
                totals[k, h] = own + (landing[k, one].astype(F32) + landing[k, two].astype(F32))
        return totals

    def ag_piece(held, k, stage, at, h):
        if stage == 0:
            if k < 3:
                return held.at[k, x, at, half(h, PART // 2)]
            return held.at[k, at, y, half(h, PART // 2)]
        if k < 3:
            return held.at[k, at, half(h, 2)]
        return held.at[k, half(h, 2), at]

    def ag_push(held, kind, k, stage, at, h, slot, to):
        piece = ag_piece(held, k, stage, at, h)
        sem = ag_recv.at[kind, stage, k % 3, int(slot not in (0, 3))]
        remote(piece, piece, ring_send.at[2 + 2 * kind + stage], sem, {ring_of(k, 1 - stage)[0]: to}).start()

    def ag_start(held, kind, group, stage):
        for first in (True, False):
            for k in group:
                name, at, plus, minus, far = ring_of(k, 1 - stage)
                for slot, h, to in ((0, 0, plus), (3, 1, minus)) if first else ((1, 1, plus), (2, 0, minus)):
                    ag_push(held, kind, k, stage, at, h, slot, to)

    def ag_like(stage, pieces):
        landing = (r2, r1)[stage]
        return landing.at[0, pl.ds(0, 4)] if pieces == 4 else landing.at[pl.ds(0, 2), pl.ds(0, 4)]

    def ag_relay(held, kind, group, stage):
        arrived(ag_like(stage, 4), ag_recv.at[kind, stage, group[0] % 3, 0])
        for k in group:
            name, at, plus, minus, far = ring_of(k, 1 - stage)
            ag_push(held, kind, k, stage, minus, 0, 4, plus)
            ag_push(held, kind, k, stage, plus, 1, 5, minus)

    def ag_finish(kind, group, stage):
        arrived(ag_like(stage, 8), ag_recv.at[kind, stage, group[0] % 3, 1])

    def core_copy(k):
        return remote(t_own.at[k], t_in.at[k], t_send, t_recv.at[k % 3], partner)

    def plane_copy(k):
        slot = lax.rem(z - k + depth, depth)
        return remote(u_b.at[k], d_in.at[slot], d_send, d_recv, {"shard": 2 * k + k % 2})

    def begin(group):
        if group != SETS[0]:
            for k in group:
                project(k)
        rs_start(group, 0)

    def turn(group):
        for (k, h), total in rs_finish(group, 0).items():
            q_f[k, 2 * h : 2 * h + 2] = total
            q_b[k, 2 * h : 2 * h + 2] = total.astype(BF16)
        rs_start(group, 1)

    def settle(group):
        if group == SETS[0]:
            m_load.wait()
            v_load.wait()
        totals = rs_finish(group, 1)
        lows = {}
        for k in group:
            lows[k] = jnp.concatenate([totals[k, 0], totals[k, 1]], axis=0) * (1.0 / math.sqrt(D))
            rough[k, x, y] = lows[k].astype(BF16)
        ag_start(rough, 0, group, 0)
        for k in group:
            first = beta_one * m_v[k] + (1.0 - beta_one) * lows[k]
            second = beta_two * v_v[k] + (1.0 - beta_two) * lows[k] * lows[k]
            m_v[k] = first
            v_v[k] = second
            step[k, x, y] = (first / bias_one / (jnp.sqrt(second / bias_two) + eps_adam)).astype(BF16)

    def widen(group):
        ag_finish(0, group, 0)
        ag_start(rough, 0, group, 1)
        ag_start(step, 1, group, 0)

    def multiply(group):
        ag_finish(0, group, 1)
        for k in group:
            t_own[k] = dot(g_v[k], rough[k].reshape(RING * RING * PART, RANK), 1, 0)

            @pl.when(core != k % 2)
            def _():
                core_copy(k).start()

        ag_relay(step, 1, group, 0)

    def scatter(group):
        for k in group:

            @pl.when(core == k % 2)
            def _():
                arrived(t_in.at[k], t_recv.at[k % 3])
                both = t_own[k] + t_in[k]

                @pl.when(z == k)
                def _():
                    s_f[...] = both

                @pl.when(z != k)
                def _():
                    u_b[k] = both.astype(BF16)
                    plane_copy(k).start()

    steps = (
        begin,
        lambda group: rs_relay(group, 0),
        turn,
        lambda group: rs_relay(group, 1),
        settle,
        lambda group: ag_relay(rough, 0, group, 0),
        widen,
        lambda group: ag_relay(rough, 0, group, 1),
        multiply,
        scatter,
    )
    for slot in range(len(steps) + LAG * (len(SETS) - 1)):
        for index in reversed(range(len(SETS))):
            if 0 <= slot - LAG * index < len(steps):
                steps[slot - LAG * index](SETS[index])

    stores = [local(m_v, m_out, store_sem.at[0]), local(v_v, v_out, store_sem.at[1])]
    for group in SETS:
        ag_finish(1, group, 0)
        ag_start(step, 1, group, 1)

    chunk = RANK // (RING * RING)
    mine = pl.ds(pl.multiple_of((x * RING + y) * chunk, chunk), chunk)
    others = [(dx, dy) for dx in (2, 1, 3, 0) for dy in (2, 1, 3, 0) if dx or dy]

    @pl.when(owner)
    def _():
        arrived(d_in.at[pl.ds(1, depth - 1)], d_recv)
        total = s_f[...]
        for slot in range(1, depth):
            total = total + d_in[slot].astype(F32)
        s_f[...] = total
        whole = split(total)
        gram[...] = dot3(whole, whole, 0, 0)
        for dx, dy in others:
            tx, ty = lax.rem(x + dx, RING), lax.rem(y + dy, RING)
            theirs = pl.ds(pl.multiple_of((tx * RING + ty) * chunk, chunk), chunk)
            remote(
                gram.at[theirs], gram_in.at[dx * RING + dy], gr_send, gr_recv, {"tensor": tx, "section": ty}
            ).start()

    for group in SETS:
        ag_relay(step, 1, group, 1)

    @pl.when(owner)
    def _():
        arrived(gram_in.at[pl.ds(1, RING * RING - 1)], gr_recv)
        total = gram[mine]
        for slot in range(1, RING * RING):
            total = total + gram_in[slot]
        gram_all[mine] = total
        for dx, dy in others:
            there = {"tensor": lax.rem(x + dx, RING), "section": lax.rem(y + dy, RING)}
            remote(gram_all.at[mine], gram_all.at[mine], ga_send, ga_recv, there).start()

    for group in SETS:
        ag_finish(1, group, 1)
        for k in group:
            product = dot(b_v[k], step[k].reshape(RING * RING * PART, RANK), 1, 1)
            del_v[k] = (-galore_gain / math.sqrt(D) * product).astype(BF16)
    stores.append(local(del_v, delta_out, store_sem.at[2]))

    @pl.when(owner)
    def _():
        arrived(gram_in.at[pl.ds(1, RING * RING - 1)], ga_recv)
        gram0 = gram_all[...]
        row_sum = jnp.sum(jnp.abs(gram0), axis=1, keepdims=True)
        bound = jnp.max(row_sum, axis=0, keepdims=True) + 1e-06
        iterate = s_f[...] / jnp.sqrt(bound)
        gram_mat = gram0 / bound
        line = lax.broadcasted_iota(jnp.int32, (RANK, RANK), 0)
        column = lax.broadcasted_iota(jnp.int32, (RANK, RANK), 1)
        identity = jnp.where(line == column, 1.5, 0.0).astype(F32)
        for turn_index in range(NS_ITERS):
            factor = split(identity - 0.5 * gram_mat)
            if turn_index + 1 < NS_ITERS:
                gram_mat = dot3(split(dot3(split(gram_mat), factor)), factor)
            iterate = dot3(split(iterate), factor)
        base[...] = (math.sqrt(D) * iterate).astype(BF16)
        for dz in (4, 3, 5, 2, 6, 1, 7):
            there = {"shard": lax.rem(z + dz, depth) * 2 + core}
            remote(base, basis_out.at[z], f_send, f_recv.at[z // 2], there).start()
        remote(base, basis_out.at[z], fc_send, fc_recv.at[z // 2], partner).start()
        local(base, basis_out.at[z], store_sem.at[3])

    for k in range(NMAT):

        @pl.when(jnp.logical_and(core == k % 2, z != k))
        def _():
            arrived(basis_out.at[k], f_recv.at[k // 2])
            remote(basis_out.at[k], basis_out.at[k], fc_send, fc_recv.at[k // 2], partner).start()

    for k in range(NMAT):

        @pl.when(core != k % 2)
        def _():
            arrived(basis_out.at[k], fc_recv.at[k // 2])

    for index, like in enumerate((r1, r2, r2, r1, r2, r1)):
        departed(like, ring_send.at[index])
    departed(t_own.at[pl.ds(0, 3)], t_send)

    @pl.when(owner)
    def _():
        departed(u_b.at[pl.ds(0, 2)], d_send)
        departed(gram_in.at[pl.ds(1, RING * RING - 1)], gr_send)
        departed(gram_in.at[pl.ds(1, RING * RING - 1)], ga_send)
        departed(d_in.at[pl.ds(1, depth - 1)], f_send)
        pltpu.make_async_copy(base, basis_out.at[z], store_sem.at[3]).wait()

    @pl.when(jnp.logical_not(owner))
    def _():
        departed(u_b.at[pl.ds(0, 3)], d_send)

    departed(u_b.at[pl.ds(0, 3)], fc_send)
    for copy in stores:
        copy.wait()


def put(*refs):
    sources, targets, sem = refs[:4], refs[4:8], refs[8]
    copies = [pltpu.make_async_copy(a, b, sem.at[i]) for i, (a, b) in enumerate(zip(sources, targets))]
    for copy in copies:
        copy.start()
    for copy in copies:
        copy.wait()


def per_device(depth, gradient, basis, moment_m, moment_v):
    dma = pltpu.SemaphoreType.DMA
    anywhere = pl.BlockSpec(memory_space=pl.ANY)
    shape = jax.ShapeDtypeStruct
    outs = (
        shape(gradient.shape, BF16),
        shape(basis.shape, BF16),
        shape(moment_m.shape, F32),
        shape(moment_v.shape, F32),
    )
    scratch = [
        pltpu.VMEM(gradient.shape, BF16),
        pltpu.VMEM(basis.shape, BF16),
        pltpu.VMEM(moment_m.shape, F32),
        pltpu.VMEM(moment_v.shape, F32),
        pltpu.VMEM((NMAT, RING, RING, PART, RANK), F32),
        pltpu.VMEM((NMAT, RING, RING, PART, RANK), BF16),
        pltpu.VMEM((NMAT, 6, 2, PART, RANK), BF16),
        pltpu.VMEM((NMAT, 2, 2, PART, RANK), BF16),
        pltpu.VMEM((NMAT, RING, PART, RANK), F32),
        pltpu.VMEM((NMAT, RING, PART, RANK), BF16),
        pltpu.VMEM((NMAT, 6, PART // 2, RANK), BF16),
        pltpu.VMEM((NMAT, 2, PART // 2, RANK), BF16),
        pltpu.VMEM((NMAT, RING, RING, PART, RANK), BF16),
        pltpu.VMEM((NMAT, RING, RING, PART, RANK), BF16),
        pltpu.VMEM((NMAT, ROWS, RANK), F32),
        pltpu.VMEM((NMAT, ROWS, RANK), F32),
        pltpu.VMEM((NMAT, ROWS, RANK), BF16),
        pltpu.VMEM((depth, ROWS, RANK), BF16),
        pltpu.VMEM((ROWS, RANK), F32),
        pltpu.VMEM((RANK, RANK), F32),
        pltpu.VMEM((RING * RING, RANK // (RING * RING), RANK), F32),
        pltpu.VMEM((RANK, RANK), F32),
        pltpu.VMEM((ROWS, RANK), BF16),
        pltpu.VMEM(gradient.shape, BF16),
        dma((NMAT + 3,)),
        dma((4,)),
        dma((6,)),
        dma((2, 3, 2)),
        dma((2, 2, 3, 2)),
        dma((3,)),
        dma((3,)),
        dma((3,)),
        dma((9,)),
    ]
    held = [pltpu.with_memory_space_constraint(a, pltpu.HBM) for a in (gradient, basis, moment_m, moment_v)]
    made = pl.pallas_call(
        functools.partial(kernel, depth),
        out_shape=outs,
        in_specs=[anywhere] * 4,
        out_specs=(anywhere,) * 4,
        scratch_shapes=scratch,
        compiler_params=pltpu.CompilerParams(
            collective_id=0, has_side_effects=True, vmem_limit_bytes=40 * 1024 * 1024
        ),
        name="galore_step",
    )(*held)
    return pl.pallas_call(
        put,
        out_shape=outs,
        in_specs=[anywhere] * 4,
        out_specs=(pl.BlockSpec(memory_space=pltpu.HBM),) * 4,
        scratch_shapes=[dma((4,))],
        compiler_params=pltpu.CompilerParams(vmem_limit_bytes=16 * 1024 * 1024),
        name="put",
    )(*made)


def solution(mesh):
    placed = (
        P(None, ("tensor", "section"), "shard"),
        P(None, ("tensor", "section"), None),
        P(None, ("shard", "tensor", "section"), None),
        P(None, ("shard", "tensor", "section"), None),
    )
    return jax.shard_map(
        functools.partial(per_device, mesh.shape["shard"] // 2),
        mesh=mesh,
        in_specs=placed,
        out_specs=placed,
        check_vma=False,
    )
```

```python
import functools
import math

import jax
import jax.numpy as jnp
from jax import lax
from jax.experimental import pallas as pl
from jax.experimental.pallas import tpu as pltpu
from jax.sharding import PartitionSpec as P

D = 2048
NS_ITERS = 4
NMAT = 6
RANK = 256
ROWS = 128
RING = 4
PART = 32
SETS = ((0, 3), (1, 4), (2, 5))

beta_one = 0.9
beta_two = 0.999
bias_one = 1.0 - 0.9**10
bias_two = 1.0 - 0.999**10
eps_adam = 1e-08
galore_gain = 4.0

F32 = jnp.float32
BF16 = jnp.bfloat16
MESH = pl.DeviceIdType.MESH


def dot(a, b, ca, cb):
    return lax.dot_general(a, b, (((ca,), (cb,)), ((), ())), preferred_element_type=F32)


def split(a):
    high = a.astype(BF16)
    return high, (a - high.astype(F32)).astype(BF16)


def dot3(a, b, ca=1, cb=0):
    (ah, al), (bh, bl) = a, b
    return dot(ah, bh, ca, cb) + (dot(ah, bl, ca, cb) + dot(al, bh, ca, cb))


def plane(k):
    return k + k // 3


def kernel(
    depth,
    g_hbm,
    b_hbm,
    m_hbm,
    v_hbm,
    delta_out,
    basis_out,
    m_out,
    v_out,
    g_v,
    b_v,
    m_v,
    v_v,
    p_f,
    p_b,
    r1,
    rel1,
    q_f,
    q_b,
    r2,
    rough,
    step,
    t_own,
    t_in,
    u_b,
    d_in,
    s_f,
    gram,
    gram_in,
    gram_all,
    base,
    del_v,
    load_sem,
    store_sem,
    ring_send,
    rs_recv,
    ag_recv,
    t_recv,
    f_recv,
    fc_recv,
    one_sem,
    told,
):
    t_send, d_send, d_recv, gr_send, gr_recv, ga_send, ga_recv, f_send, fc_send = (one_sem.at[i] for i in range(9))
    shard = lax.axis_index("shard")
    x = lax.axis_index("tensor")
    y = lax.axis_index("section")
    z, core = shard // 2, lax.rem(shard, 2)
    partner = {"shard": z * 2 + (1 - core)}
    places = {"tensor": x, "section": y}
    matrix = z - z // 4
    owner = jnp.logical_and(lax.rem(z, 4) != 3, core == lax.rem(matrix, 2))

    def local(src, dst, sem):
        copy = pltpu.make_async_copy(src, dst, sem)
        copy.start()
        return copy

    def remote(src, dst, send_sem, recv_sem, where):
        return pltpu.make_async_remote_copy(
            src_ref=src,
            dst_ref=dst,
            send_sem=send_sem,
            recv_sem=recv_sem,
            device_id=where,
            device_id_type=MESH,
        )

    def arrived(like, sem):
        remote(like, like, sem, sem, partner).wait_recv()

    def departed(like, sem):
        remote(like, like, sem, sem, partner).wait_send()

    barrier = pltpu.get_barrier_semaphore()
    peers = [
        {"tensor": lax.rem(x + dx, RING), "section": lax.rem(y + dy, RING)}
        for dx in range(RING)
        for dy in range(RING)
        if (dx == 0) != (dy == 0) and 2 not in (dx, dy)
    ]
    beside = [{"shard": lax.rem(z + dz, depth) * 2 + core} for dz in (1, depth - 1)]
    peers += beside
    peers.append(partner)
    for there in peers:
        pl.semaphore_signal(barrier, inc=1, device_id=there, device_id_type=MESH)

    b_load = local(b_hbm, b_v, load_sem.at[NMAT])
    g_load = {k: local(g_hbm.at[k], g_v.at[k], load_sem.at[k]) for group in SETS for k in group}
    m_load = local(m_hbm, m_v, load_sem.at[NMAT + 1])
    v_load = local(v_hbm, v_v, load_sem.at[NMAT + 2])

    def project(k):
        g_load[k].wait()
        part = dot(g_v[k], b_v[k], 0, 0).reshape(RING, RING, PART, RANK)
        p_f[k] = part
        p_b[k] = part.astype(BF16)

    b_load.wait()
    for group in SETS:
        for k in group:
            project(k)
    pl.semaphore_wait(barrier, len(peers))

    def tell(turn):
        for there in beside:
            pl.semaphore_signal(told.at[turn], inc=1, device_id=there, device_id_type=MESH)

    def hear(turn):
        pl.semaphore_wait(told.at[turn], len(beside))
        if turn < 2:
            tell(turn + 1)

    tell(0)

    def ring_of(k, stage):
        name = ("tensor", "section")[(stage + (k >= 3)) % 2]
        at = places[name]
        plus, minus, far = (lax.rem(at + i, RING) for i in (1, 3, 2))
        return name, at, plus, minus, far

    def half(h, size):
        return pl.ds(h * size, size)

    def across(k, stage, landing, sem, sources):
        name, at, plus, minus, far = ring_of(k, stage)
        for slot, to in enumerate((far, plus, minus)):
            remote(sources(to), landing(slot), ring_send.at[sem[0]], sem[1], {name: to}).start()

    def piece(source, k, at, h):
        if k < 3:
            return source.at[k, at, half(h, 2)]
        return source.at[k, half(h, 2), at]

    def rs_push(k, src, slot, to):
        sem = rs_recv.at[k % 3, int(slot >= 2)]
        remote(src, r1.at[k, slot], ring_send.at[0], sem, {ring_of(k, 0)[0]: to}).start()

    def rs_begin(group):
        for k in group:
            name, at, plus, minus, far = ring_of(k, 0)
            rs_push(k, piece(p_b, k, far, 0), 0, plus)
            rs_push(k, piece(p_b, k, far, 1), 1, minus)

    def rs_direct(group):
        for k in group:
            name, at, plus, minus, far = ring_of(k, 0)
            rs_push(k, piece(p_b, k, plus, 1), 2, plus)
            rs_push(k, piece(p_b, k, minus, 0), 3, minus)

    def rs_relay(group):
        arrived(r1.at[0, pl.ds(0, 4)], rs_recv.at[group[0] % 3, 0])
        for k in group:
            name, at, plus, minus, far = ring_of(k, 0)
            for slot, to in ((0, plus), (1, minus)):
                own = piece(p_f, k, to, slot)[...]
                rel1[k, slot] = (own + r1[k, slot].astype(F32)).astype(BF16)
                rs_push(k, rel1.at[k, slot], slot + 4, to)

    def rs_turn(group):
        arrived(r1.at[pl.ds(0, 2), pl.ds(0, 4)], rs_recv.at[group[0] % 3, 1])
        for k in group:
            at = ring_of(k, 0)[1]
            for h, (one, two) in enumerate(((3, 4), (2, 5))):
                own = piece(p_f, k, at, h)[...]
                total = own + (r1[k, one].astype(F32) + r1[k, two].astype(F32))
                q_f[k, 2 * h : 2 * h + 2] = total
                q_b[k, 2 * h : 2 * h + 2] = total.astype(BF16)
            across(k, 1, lambda slot: r2.at[k, slot], (1, rs_recv.at[k % 3, 2]), lambda to: q_b.at[k, to])

    def ag_begin(held, kind, group):
        for k in group:
            own = held.at[k, x, y]
            across(k, 1, lambda slot: own, (2 + 2 * kind, ag_recv.at[kind, k % 3, 2]), lambda to: own)

    def ag_push(held, kind, k, at, h, slot, to):
        sem = ag_recv.at[kind, k % 3, int(slot not in (0, 3))]
        part = piece(held, k, at, h)
        remote(part, part, ring_send.at[3 + 2 * kind], sem, {ring_of(k, 0)[0]: to}).start()

    def ag_turn(held, kind, group):
        arrived(r2.at[pl.ds(0, 2)], ag_recv.at[kind, group[0] % 3, 2])
        for k in group:
            name, at, plus, minus, far = ring_of(k, 0)
            ag_push(held, kind, k, at, 0, 0, plus)
            ag_push(held, kind, k, at, 1, 3, minus)

    def ag_direct(held, kind, group):
        for k in group:
            name, at, plus, minus, far = ring_of(k, 0)
            ag_push(held, kind, k, at, 1, 1, plus)
            ag_push(held, kind, k, at, 0, 2, minus)

    def ag_relay(held, kind, group):
        arrived(r1.at[0, pl.ds(0, 4)], ag_recv.at[kind, group[0] % 3, 0])
        for k in group:
            name, at, plus, minus, far = ring_of(k, 0)
            ag_push(held, kind, k, minus, 0, 4, plus)
            ag_push(held, kind, k, plus, 1, 5, minus)

    def ag_finish(kind, group):
        arrived(r1.at[pl.ds(0, 2), pl.ds(0, 4)], ag_recv.at[kind, group[0] % 3, 1])

    def core_copy(k):
        return remote(t_own.at[k], t_in.at[k], t_send, t_recv.at[k % 3], partner)

    def plane_copy(k):
        slot = lax.rem(z - plane(k) + depth, depth)
        return remote(u_b.at[k], d_in.at[slot], d_send, d_recv, {"shard": 2 * plane(k) + k % 2})

    def settle(group):
        arrived(r2.at[pl.ds(0, 2)], rs_recv.at[group[0] % 3, 2])
        lows = {}
        for k in group:
            own = q_f[k, ring_of(k, 1)[1]]
            total = own + (r2[k, 0].astype(F32) + r2[k, 1].astype(F32) + r2[k, 2].astype(F32))
            lows[k] = total * (1.0 / math.sqrt(D))
            rough[k, x, y] = lows[k].astype(BF16)
        ag_begin(rough, 0, group)
        if group == SETS[0]:
            m_load.wait()
            v_load.wait()
        for k in group:
            first = beta_one * m_v[k] + (1.0 - beta_one) * lows[k]
            second = beta_two * v_v[k] + (1.0 - beta_two) * lows[k] * lows[k]
            m_v[k] = first
            v_v[k] = second
            step[k, x, y] = (first / bias_one / (jnp.sqrt(second / bias_two) + eps_adam)).astype(BF16)

    def multiply(group):
        ag_finish(0, group)
        for k in group:
            t_own[k] = dot(g_v[k], rough[k].reshape(RING * RING * PART, RANK), 1, 0)

            @pl.when(core != k % 2)
            def _():
                core_copy(k).start()

    def scatter(group):
        for k in group:

            @pl.when(core == k % 2)
            def _():
                arrived(t_in.at[k], t_recv.at[k % 3])
                both = t_own[k] + t_in[k]

                @pl.when(z == plane(k))
                def _():
                    s_f[...] = both

                @pl.when(z != plane(k))
                def _():
                    u_b[k] = both.astype(BF16)
                    plane_copy(k).start()

    for task in (
        rs_begin,
        rs_direct,
        rs_relay,
        rs_turn,
        settle,
        functools.partial(ag_turn, rough, 0),
        functools.partial(ag_direct, rough, 0),
        functools.partial(ag_relay, rough, 0),
        functools.partial(ag_begin, step, 1),
    ):
        for group in SETS:
            task(group)
        if task in (rs_relay, settle):
            hear(int(task is settle))
    hear(2)
    multiply(SETS[0])
    multiply(SETS[1])
    scatter(SETS[0])
    multiply(SETS[2])
    scatter(SETS[1])
    scatter(SETS[2])
    for task in (functools.partial(ag_turn, step, 1), functools.partial(ag_direct, step, 1)):
        for group in SETS:
            task(group)

    stores = [local(m_v, m_out, store_sem.at[0]), local(v_v, v_out, store_sem.at[1])]
    chunk = RANK // (RING * RING)
    mine = pl.ds(pl.multiple_of((x * RING + y) * chunk, chunk), chunk)
    others = [(dx, dy) for dx in (2, 1, 3, 0) for dy in (2, 1, 3, 0) if dx or dy]

    @pl.when(owner)
    def _():
        arrived(d_in.at[pl.ds(1, depth - 1)], d_recv)
        total = s_f[...]
        for slot in range(1, depth):
            total = total + d_in[slot].astype(F32)
        s_f[...] = total
        whole = split(total)
        gram[...] = dot3(whole, whole, 0, 0)
        for dx, dy in others:
            tx, ty = lax.rem(x + dx, RING), lax.rem(y + dy, RING)
            theirs = pl.ds(pl.multiple_of((tx * RING + ty) * chunk, chunk), chunk)
            remote(
                gram.at[theirs], gram_in.at[dx * RING + dy], gr_send, gr_recv, {"tensor": tx, "section": ty}
            ).start()

    for group in SETS:
        ag_relay(step, 1, group)

    @pl.when(owner)
    def _():
        arrived(gram_in.at[pl.ds(1, RING * RING - 1)], gr_recv)
        total = gram[mine]
        for slot in range(1, RING * RING):
            total = total + gram_in[slot]
        gram_all[mine] = total
        for dx, dy in others:
            there = {"tensor": lax.rem(x + dx, RING), "section": lax.rem(y + dy, RING)}
            remote(gram_all.at[mine], gram_all.at[mine], ga_send, ga_recv, there).start()

    for group in SETS:
        ag_finish(1, group)
        for k in group:
            product = dot(b_v[k], step[k].reshape(RING * RING * PART, RANK), 1, 1)
            del_v[k] = (-galore_gain / math.sqrt(D) * product).astype(BF16)
    stores.append(local(del_v, delta_out, store_sem.at[2]))

    @pl.when(owner)
    def _():
        arrived(gram_in.at[pl.ds(1, RING * RING - 1)], ga_recv)
        gram0 = gram_all[...]
        row_sum = jnp.sum(jnp.abs(gram0), axis=1, keepdims=True)
        bound = jnp.max(row_sum, axis=0, keepdims=True) + 1e-06
        iterate = s_f[...] / jnp.sqrt(bound)
        gram_mat = gram0 / bound
        line = lax.broadcasted_iota(jnp.int32, (RANK, RANK), 0)
        column = lax.broadcasted_iota(jnp.int32, (RANK, RANK), 1)
        identity = jnp.where(line == column, 1.5, 0.0).astype(F32)
        for turn_index in range(NS_ITERS):
            factor = split(identity - 0.5 * gram_mat)
            if turn_index + 1 < NS_ITERS:
                gram_mat = dot3(split(dot3(split(gram_mat), factor)), factor)
            iterate = dot3(split(iterate), factor)
        base[...] = (math.sqrt(D) * iterate).astype(BF16)
        for dz in (4, 3, 5, 2, 6, 1, 7):
            there = {"shard": lax.rem(z + dz, depth) * 2 + core}
            remote(base, basis_out.at[matrix], f_send, f_recv.at[matrix // 2], there).start()
        remote(base, basis_out.at[matrix], fc_send, fc_recv.at[matrix // 2], partner).start()
        local(base, basis_out.at[matrix], store_sem.at[3])

    for k in range(NMAT):

        @pl.when(jnp.logical_and(core == k % 2, z != plane(k)))
        def _():
            arrived(basis_out.at[k], f_recv.at[k // 2])
            remote(basis_out.at[k], basis_out.at[k], fc_send, fc_recv.at[k // 2], partner).start()

    for k in range(NMAT):

        @pl.when(core != k % 2)
        def _():
            arrived(basis_out.at[k], fc_recv.at[k // 2])

    for index, like in enumerate((r1, r2, r2, r1, r2, r1)):
        departed(like, ring_send.at[index])
    departed(t_own.at[pl.ds(0, 3)], t_send)

    @pl.when(owner)
    def _():
        departed(u_b.at[pl.ds(0, 2)], d_send)
        departed(gram_in.at[pl.ds(1, RING * RING - 1)], gr_send)
        departed(gram_in.at[pl.ds(1, RING * RING - 1)], ga_send)
        departed(d_in.at[pl.ds(1, depth - 1)], f_send)
        pltpu.make_async_copy(base, basis_out.at[matrix], store_sem.at[3]).wait()

    @pl.when(jnp.logical_not(owner))
    def _():
        departed(u_b.at[pl.ds(0, 3)], d_send)

    departed(u_b.at[pl.ds(0, 3)], fc_send)
    for copy in stores:
        copy.wait()


def put(*refs):
    sources, targets, sem = refs[:4], refs[4:8], refs[8]
    copies = [pltpu.make_async_copy(a, b, sem.at[i]) for i, (a, b) in enumerate(zip(sources, targets))]
    for copy in copies:
        copy.start()
    for copy in copies:
        copy.wait()


def per_device(depth, gradient, basis, moment_m, moment_v):
    dma = pltpu.SemaphoreType.DMA
    anywhere = pl.BlockSpec(memory_space=pl.ANY)
    shape = jax.ShapeDtypeStruct
    outs = (
        shape(gradient.shape, BF16),
        shape(basis.shape, BF16),
        shape(moment_m.shape, F32),
        shape(moment_v.shape, F32),
    )
    scratch = [
        pltpu.VMEM(gradient.shape, BF16),
        pltpu.VMEM(basis.shape, BF16),
        pltpu.VMEM(moment_m.shape, F32),
        pltpu.VMEM(moment_v.shape, F32),
        pltpu.VMEM((NMAT, RING, RING, PART, RANK), F32),
        pltpu.VMEM((NMAT, RING, RING, PART, RANK), BF16),
        pltpu.VMEM((NMAT, 6, 2, PART, RANK), BF16),
        pltpu.VMEM((NMAT, 2, 2, PART, RANK), BF16),
        pltpu.VMEM((NMAT, RING, PART, RANK), F32),
        pltpu.VMEM((NMAT, RING, PART, RANK), BF16),
        pltpu.VMEM((NMAT, 3, PART, RANK), BF16),
        pltpu.VMEM((NMAT, RING, RING, PART, RANK), BF16),
        pltpu.VMEM((NMAT, RING, RING, PART, RANK), BF16),
        pltpu.VMEM((NMAT, ROWS, RANK), F32),
        pltpu.VMEM((NMAT, ROWS, RANK), F32),
        pltpu.VMEM((NMAT, ROWS, RANK), BF16),
        pltpu.VMEM((depth, ROWS, RANK), BF16),
        pltpu.VMEM((ROWS, RANK), F32),
        pltpu.VMEM((RANK, RANK), F32),
        pltpu.VMEM((RING * RING, RANK // (RING * RING), RANK), F32),
        pltpu.VMEM((RANK, RANK), F32),
        pltpu.VMEM((ROWS, RANK), BF16),
        pltpu.VMEM(gradient.shape, BF16),
        dma((NMAT + 3,)),
        dma((4,)),
        dma((6,)),
        dma((3, 3)),
        dma((2, 3, 3)),
        dma((3,)),
        dma((3,)),
        dma((3,)),
        dma((9,)),
        pltpu.SemaphoreType.REGULAR((3,)),
    ]
    held = [pltpu.with_memory_space_constraint(a, pltpu.HBM) for a in (gradient, basis, moment_m, moment_v)]
    made = pl.pallas_call(
        functools.partial(kernel, depth),
        out_shape=outs,
        in_specs=[anywhere] * 4,
        out_specs=(anywhere,) * 4,
        scratch_shapes=scratch,
        compiler_params=pltpu.CompilerParams(
            collective_id=0, has_side_effects=True, vmem_limit_bytes=40 * 1024 * 1024
        ),
        name="galore_step",
    )(*held)
    return pl.pallas_call(
        put,
        out_shape=outs,
        in_specs=[anywhere] * 4,
        out_specs=(pl.BlockSpec(memory_space=pltpu.HBM),) * 4,
        scratch_shapes=[dma((4,))],
        compiler_params=pltpu.CompilerParams(vmem_limit_bytes=16 * 1024 * 1024),
        name="put",
    )(*made)


def solution(mesh):
    placed = (
        P(None, ("tensor", "section"), "shard"),
        P(None, ("tensor", "section"), None),
        P(None, ("shard", "tensor", "section"), None),
        P(None, ("shard", "tensor", "section"), None),
    )
    return jax.shard_map(
        functools.partial(per_device, mesh.shape["shard"] // 2),
        mesh=mesh,
        in_specs=placed,
        out_specs=placed,
        check_vma=False,
    )
```

```python
import functools
import math

import jax
import jax.numpy as jnp
from jax import lax
from jax.experimental import pallas as pl
from jax.experimental.pallas import tpu as pltpu
from jax.sharding import PartitionSpec as P

D = 2048
NS_ITERS = 4
NMAT = 6
RANK = 256
ROWS = 128
RING = 4
PART = 32
SETS = ((0, 3), (1, 4), (2, 5))

beta_one = 0.9
beta_two = 0.999
bias_one = 1.0 - 0.9**10
bias_two = 1.0 - 0.999**10
eps_adam = 1e-08
galore_gain = 4.0

F32 = jnp.float32
BF16 = jnp.bfloat16
MESH = pl.DeviceIdType.MESH


def dot(a, b, ca, cb):
    return lax.dot_general(a, b, (((ca,), (cb,)), ((), ())), preferred_element_type=F32)


def split(a):
    high = a.astype(BF16)
    return high, (a - high.astype(F32)).astype(BF16)


def dot3(a, b, ca=1, cb=0):
    (ah, al), (bh, bl) = a, b
    return dot(ah, bh, ca, cb) + (dot(ah, bl, ca, cb) + dot(al, bh, ca, cb))


def plane(k):
    return k + k // 3


def kernel(
    depth,
    g_hbm,
    b_hbm,
    m_hbm,
    v_hbm,
    delta_out,
    basis_out,
    m_out,
    v_out,
    g_v,
    b_v,
    m_v,
    v_v,
    p_f,
    p_b,
    r1,
    rel1,
    q_f,
    q_b,
    r2,
    rough,
    step,
    t_own,
    t_in,
    u_b,
    d_in,
    s_f,
    gram,
    gram_in,
    gram_all,
    base,
    del_v,
    load_sem,
    store_sem,
    ring_send,
    rs_recv,
    ag_recv,
    t_recv,
    f_send,
    f_recv,
    fc_recv,
    one_sem,
    told,
):
    t_send, d_send, d_recv, gr_send, gr_recv, ga_send, ga_recv, fc_send = (one_sem.at[i] for i in range(8))
    shard = lax.axis_index("shard")
    x = lax.axis_index("tensor")
    y = lax.axis_index("section")
    z, core = shard // 2, lax.rem(shard, 2)
    partner = {"shard": z * 2 + (1 - core)}
    places = {"tensor": x, "section": y}
    matrix = z - z // 4
    owner = jnp.logical_and(lax.rem(z, 4) != 3, core == lax.rem(matrix, 2))

    def local(src, dst, sem):
        copy = pltpu.make_async_copy(src, dst, sem)
        copy.start()
        return copy

    def remote(src, dst, send_sem, recv_sem, where):
        return pltpu.make_async_remote_copy(
            src_ref=src,
            dst_ref=dst,
            send_sem=send_sem,
            recv_sem=recv_sem,
            device_id=where,
            device_id_type=MESH,
        )

    def arrived(like, sem):
        remote(like, like, sem, sem, partner).wait_recv()

    def departed(like, sem):
        remote(like, like, sem, sem, partner).wait_send()

    barrier = pltpu.get_barrier_semaphore()
    peers = [
        {"tensor": lax.rem(x + dx, RING), "section": lax.rem(y + dy, RING)}
        for dx in range(RING)
        for dy in range(RING)
        if (dx == 0) != (dy == 0) and 2 not in (dx, dy)
    ]
    beside = [{"shard": lax.rem(z + dz, depth) * 2 + core} for dz in (1, depth - 1)]
    peers += beside
    peers.append(partner)
    for there in peers:
        pl.semaphore_signal(barrier, inc=1, device_id=there, device_id_type=MESH)

    b_load = local(b_hbm, b_v, load_sem.at[NMAT])
    g_load = {k: local(g_hbm.at[k], g_v.at[k], load_sem.at[k]) for group in SETS for k in group}
    m_load = local(m_hbm, m_v, load_sem.at[NMAT + 1])
    v_load = local(v_hbm, v_v, load_sem.at[NMAT + 2])

    def project(k):
        g_load[k].wait()
        part = dot(g_v[k], b_v[k], 0, 0).reshape(RING, RING, PART, RANK)
        p_f[k] = part
        p_b[k] = part.astype(BF16)

    b_load.wait()
    for group in SETS:
        for k in group:
            project(k)
    pl.semaphore_wait(barrier, len(peers))

    def tell(turn):
        for there in beside:
            pl.semaphore_signal(told.at[turn], inc=1, device_id=there, device_id_type=MESH)

    def hear(turn):
        pl.semaphore_wait(told.at[turn], len(beside))
        if turn < 2:
            tell(turn + 1)

    tell(0)

    def ring_of(k, stage):
        name = ("tensor", "section")[(stage + (k >= 3)) % 2]
        at = places[name]
        plus, minus, far = (lax.rem(at + i, RING) for i in (1, 3, 2))
        return name, at, plus, minus, far

    def half(h, size):
        return pl.ds(h * size, size)

    def across(k, stage, landing, sem, sources):
        name, at, plus, minus, far = ring_of(k, stage)
        for slot, to in enumerate((far, plus, minus)):
            remote(sources(to), landing(slot), ring_send.at[sem[0]], sem[1], {name: to}).start()

    def piece(source, k, at, h):
        if k < 3:
            return source.at[k, at, half(h, 2)]
        return source.at[k, half(h, 2), at]

    def rs_push(k, src, slot, to):
        sem = rs_recv.at[k % 3, int(slot >= 2)]
        remote(src, r1.at[k, slot], ring_send.at[0], sem, {ring_of(k, 0)[0]: to}).start()

    def rs_begin(group):
        for k in group:
            name, at, plus, minus, far = ring_of(k, 0)
            rs_push(k, piece(p_b, k, far, 0), 0, plus)
            rs_push(k, piece(p_b, k, far, 1), 1, minus)

    def rs_direct(group):
        for k in group:
            name, at, plus, minus, far = ring_of(k, 0)
            rs_push(k, piece(p_b, k, plus, 1), 2, plus)
            rs_push(k, piece(p_b, k, minus, 0), 3, minus)

    def rs_relay(group):
        arrived(r1.at[0, pl.ds(0, 4)], rs_recv.at[group[0] % 3, 0])
        for k in group:
            name, at, plus, minus, far = ring_of(k, 0)
            for slot, to in ((0, plus), (1, minus)):
                own = piece(p_f, k, to, slot)[...]
                rel1[k, slot] = (own + r1[k, slot].astype(F32)).astype(BF16)
                rs_push(k, rel1.at[k, slot], slot + 4, to)

    def rs_turn(group):
        arrived(r1.at[pl.ds(0, 2), pl.ds(0, 4)], rs_recv.at[group[0] % 3, 1])
        for k in group:
            at = ring_of(k, 0)[1]
            for h, (one, two) in enumerate(((3, 4), (2, 5))):
                own = piece(p_f, k, at, h)[...]
                total = own + (r1[k, one].astype(F32) + r1[k, two].astype(F32))
                q_f[k, 2 * h : 2 * h + 2] = total
                q_b[k, 2 * h : 2 * h + 2] = total.astype(BF16)
            across(k, 1, lambda slot: r2.at[k, slot], (1, rs_recv.at[k % 3, 2]), lambda to: q_b.at[k, to])

    def ag_begin(held, kind, group):
        for k in group:
            own = held.at[k, x, y]
            across(k, 1, lambda slot: own, (2 + 2 * kind, ag_recv.at[kind, k % 3, 2]), lambda to: own)

    def ag_push(held, kind, k, at, h, slot, to):
        sem = ag_recv.at[kind, k % 3, int(slot not in (0, 3))]
        part = piece(held, k, at, h)
        remote(part, part, ring_send.at[3 + 2 * kind], sem, {ring_of(k, 0)[0]: to}).start()

    def ag_turn(held, kind, group):
        arrived(r2.at[pl.ds(0, 2)], ag_recv.at[kind, group[0] % 3, 2])
        for k in group:
            name, at, plus, minus, far = ring_of(k, 0)
            ag_push(held, kind, k, at, 0, 0, plus)
            ag_push(held, kind, k, at, 1, 3, minus)

    def ag_direct(held, kind, group):
        for k in group:
            name, at, plus, minus, far = ring_of(k, 0)
            ag_push(held, kind, k, at, 1, 1, plus)
            ag_push(held, kind, k, at, 0, 2, minus)

    def ag_relay(held, kind, group):
        arrived(r1.at[0, pl.ds(0, 4)], ag_recv.at[kind, group[0] % 3, 0])
        for k in group:
            name, at, plus, minus, far = ring_of(k, 0)
            ag_push(held, kind, k, minus, 0, 4, plus)
            ag_push(held, kind, k, plus, 1, 5, minus)

    def ag_full(held, kind, group):
        arrived(r2.at[pl.ds(0, 2)], ag_recv.at[kind, group[0] % 3, 2])
        for k in group:
            name, at, plus, minus, far = ring_of(k, 0)
            for to in (far, plus, minus):
                for h in range(2):
                    part = piece(held, k, at, h)
                    remote(part, part, ring_send.at[3 + 2 * kind], ag_recv.at[kind, k % 3, 1], {name: to}).start()

    def ag_whole(kind, group):
        arrived(r1.at[pl.ds(0, 2)], ag_recv.at[kind, group[0] % 3, 1])

    def ag_finish(kind, group):
        arrived(r1.at[pl.ds(0, 2), pl.ds(0, 4)], ag_recv.at[kind, group[0] % 3, 1])

    def core_copy(k):
        return remote(t_own.at[k], t_in.at[k], t_send, t_recv.at[k % 3], partner)

    def plane_copy(k):
        slot = lax.rem(z - plane(k) + depth, depth)
        return remote(u_b.at[k], d_in.at[slot], d_send, d_recv, {"shard": 2 * plane(k) + k % 2})

    def settle(group):
        arrived(r2.at[pl.ds(0, 2)], rs_recv.at[group[0] % 3, 2])
        lows = {}
        for k in group:
            own = q_f[k, ring_of(k, 1)[1]]
            total = own + (r2[k, 0].astype(F32) + r2[k, 1].astype(F32) + r2[k, 2].astype(F32))
            lows[k] = total * (1.0 / math.sqrt(D))
            rough[k, x, y] = lows[k].astype(BF16)
        ag_begin(rough, 0, group)
        if group == SETS[0]:
            m_load.wait()
            v_load.wait()
        for k in group:
            first = beta_one * m_v[k] + (1.0 - beta_one) * lows[k]
            second = beta_two * v_v[k] + (1.0 - beta_two) * lows[k] * lows[k]
            m_v[k] = first
            v_v[k] = second
            step[k, x, y] = (first / bias_one / (jnp.sqrt(second / bias_two) + eps_adam)).astype(BF16)

    def multiply(group):
        ag_whole(0, group)

        def product(k):
            t_own[k] = dot(g_v[k], rough[k].reshape(RING * RING * PART, RANK), 1, 0)

        for parity in range(2):
            kept, given = sorted(group, key=lambda k: k % 2 != parity)

            @pl.when(core == parity)
            def _():
                product(given)
                core_copy(given).start()
                product(kept)

    def scatter(group):
        for k in group:

            @pl.when(core == k % 2)
            def _():
                arrived(t_in.at[k], t_recv.at[k % 3])
                both = t_own[k] + t_in[k]

                @pl.when(z == plane(k))
                def _():
                    s_f[...] = both

                @pl.when(z != plane(k))
                def _():
                    u_b[k] = both.astype(BF16)
                    plane_copy(k).start()

    for task in (
        rs_begin,
        rs_direct,
        rs_relay,
        rs_turn,
        settle,
        functools.partial(ag_full, rough, 0),
        functools.partial(ag_begin, step, 1),
    ):
        for group in SETS:
            task(group)
        if task in (rs_relay, settle):
            hear(int(task is settle))
    hear(2)
    for group in SETS:
        multiply(group)
        scatter(group)
    for task in (functools.partial(ag_turn, step, 1), functools.partial(ag_direct, step, 1)):
        for group in SETS:
            task(group)

    stores = [local(m_v, m_out, store_sem.at[0]), local(v_v, v_out, store_sem.at[1])]
    chunk = RANK // (RING * RING)
    mine = pl.ds(pl.multiple_of((x * RING + y) * chunk, chunk), chunk)
    others = [(dx, dy) for dx in (2, 1, 3, 0) for dy in (2, 1, 3, 0) if dx or dy]

    @pl.when(owner)
    def _():
        arrived(d_in.at[pl.ds(1, depth - 1)], d_recv)
        total = s_f[...]
        for slot in range(1, depth):
            total = total + d_in[slot].astype(F32)
        s_f[...] = total
        whole = split(total)
        gram[...] = dot3(whole, whole, 0, 0)
        for dx, dy in others:
            tx, ty = lax.rem(x + dx, RING), lax.rem(y + dy, RING)
            theirs = pl.ds(pl.multiple_of((tx * RING + ty) * chunk, chunk), chunk)
            remote(
                gram.at[theirs], gram_in.at[dx * RING + dy], gr_send, gr_recv, {"tensor": tx, "section": ty}
            ).start()

    for group in SETS:
        ag_relay(step, 1, group)

    @pl.when(owner)
    def _():
        arrived(gram_in.at[pl.ds(1, RING * RING - 1)], gr_recv)
        total = gram[mine]
        for slot in range(1, RING * RING):
            total = total + gram_in[slot]
        gram_all[mine] = total
        for dx, dy in others:
            there = {"tensor": lax.rem(x + dx, RING), "section": lax.rem(y + dy, RING)}
            remote(gram_all.at[mine], gram_all.at[mine], ga_send, ga_recv, there).start()

    for group in SETS:
        ag_finish(1, group)
        for k in group:
            product = dot(b_v[k], step[k].reshape(RING * RING * PART, RANK), 1, 1)
            del_v[k] = (-galore_gain / math.sqrt(D) * product).astype(BF16)
    stores.append(local(del_v, delta_out, store_sem.at[2]))

    @pl.when(owner)
    def _():
        arrived(gram_in.at[pl.ds(1, RING * RING - 1)], ga_recv)
        gram0 = gram_all[...]
        row_sum = jnp.sum(jnp.abs(gram0), axis=1, keepdims=True)
        bound = jnp.max(row_sum, axis=0, keepdims=True) + 1e-06
        iterate = s_f[...] / jnp.sqrt(bound)
        gram_mat = gram0 / bound
        line = lax.broadcasted_iota(jnp.int32, (RANK, RANK), 0)
        column = lax.broadcasted_iota(jnp.int32, (RANK, RANK), 1)
        identity = jnp.where(line == column, 1.5, 0.0).astype(F32)
        for turn_index in range(NS_ITERS):
            factor = split(identity - 0.5 * gram_mat)
            if turn_index + 1 < NS_ITERS:
                gram_mat = dot3(split(dot3(split(gram_mat), factor)), factor)
            iterate = dot3(split(iterate), factor)
        base[...] = (math.sqrt(D) * iterate).astype(BF16)
        for dz in (3, 5, 2, 6, 1, 7):
            there = {"shard": lax.rem(z + dz, depth) * 2 + core}
            remote(base, basis_out.at[matrix], f_send.at[matrix // 2], f_recv.at[matrix // 2], there).start()
        remote(base, basis_out.at[matrix], fc_send, fc_recv.at[matrix // 2], partner).start()
        local(base, basis_out.at[matrix], store_sem.at[3])

    def pass_on(k, offset):
        for source, target, part in ((3, 4, 0), (5, 4, 1)):
            if source == offset:
                rows = pl.ds(0, ROWS) if part is None else half(part, ROWS // 2)
                there = {"shard": lax.rem(z + (target - source) + depth, depth) * 2 + core}
                held = basis_out.at[k, rows]
                remote(held, held, f_send.at[k // 2], f_recv.at[k // 2], there).start()

    ordered = [k for group in SETS for k in group]
    for k in ordered:
        offset = lax.rem(z - plane(k) + depth, depth)

        @pl.when(jnp.logical_and(core == k % 2, offset != 0))
        def _():
            arrived(basis_out.at[k], f_recv.at[k // 2])
            for source in (3, 5):

                @pl.when(offset == source)
                def _():
                    pass_on(k, source)

            remote(basis_out.at[k], basis_out.at[k], fc_send, fc_recv.at[k // 2], partner).start()

    for k in ordered:

        @pl.when(core != k % 2)
        def _():
            arrived(basis_out.at[k], fc_recv.at[k // 2])

    for index, like in enumerate((r1, r2, r2, r1, r2, r1)):
        departed(like, ring_send.at[index])
    departed(t_own.at[pl.ds(0, 3)], t_send)

    @pl.when(owner)
    def _():
        departed(u_b.at[pl.ds(0, 2)], d_send)
        departed(gram_in.at[pl.ds(1, RING * RING - 1)], gr_send)
        departed(gram_in.at[pl.ds(1, RING * RING - 1)], ga_send)
        departed(d_in.at[pl.ds(0, 6)], f_send.at[matrix // 2])
        pltpu.make_async_copy(base, basis_out.at[matrix], store_sem.at[3]).wait()

    @pl.when(jnp.logical_not(owner))
    def _():
        departed(u_b.at[pl.ds(0, 3)], d_send)

    for k in range(NMAT):
        offset = lax.rem(z - plane(k) + depth, depth)

        @pl.when(jnp.logical_and(core == k % 2, jnp.logical_or(offset == 3, offset == 5)))
        def _():
            departed(r2.at[0:1, pl.ds(0, 2)], f_send.at[k // 2])

    departed(u_b.at[pl.ds(0, 3)], fc_send)
    for copy in stores:
        copy.wait()


def put(*refs):
    sources, targets, sem = refs[:4], refs[4:8], refs[8]
    copies = [pltpu.make_async_copy(a, b, sem.at[i]) for i, (a, b) in enumerate(zip(sources, targets))]
    for copy in copies:
        copy.start()
    for copy in copies:
        copy.wait()


def per_device(depth, gradient, basis, moment_m, moment_v):
    dma = pltpu.SemaphoreType.DMA
    anywhere = pl.BlockSpec(memory_space=pl.ANY)
    shape = jax.ShapeDtypeStruct
    outs = (
        shape(gradient.shape, BF16),
        shape(basis.shape, BF16),
        shape(moment_m.shape, F32),
        shape(moment_v.shape, F32),
    )
    scratch = [
        pltpu.VMEM(gradient.shape, BF16),
        pltpu.VMEM(basis.shape, BF16),
        pltpu.VMEM(moment_m.shape, F32),
        pltpu.VMEM(moment_v.shape, F32),
        pltpu.VMEM((NMAT, RING, RING, PART, RANK), F32),
        pltpu.VMEM((NMAT, RING, RING, PART, RANK), BF16),
        pltpu.VMEM((NMAT, 6, 2, PART, RANK), BF16),
        pltpu.VMEM((NMAT, 2, 2, PART, RANK), BF16),
        pltpu.VMEM((NMAT, RING, PART, RANK), F32),
        pltpu.VMEM((NMAT, RING, PART, RANK), BF16),
        pltpu.VMEM((NMAT, 3, PART, RANK), BF16),
        pltpu.VMEM((NMAT, RING, RING, PART, RANK), BF16),
        pltpu.VMEM((NMAT, RING, RING, PART, RANK), BF16),
        pltpu.VMEM((NMAT, ROWS, RANK), F32),
        pltpu.VMEM((NMAT, ROWS, RANK), F32),
        pltpu.VMEM((NMAT, ROWS, RANK), BF16),
        pltpu.VMEM((depth, ROWS, RANK), BF16),
        pltpu.VMEM((ROWS, RANK), F32),
        pltpu.VMEM((RANK, RANK), F32),
        pltpu.VMEM((RING * RING, RANK // (RING * RING), RANK), F32),
        pltpu.VMEM((RANK, RANK), F32),
        pltpu.VMEM((ROWS, RANK), BF16),
        pltpu.VMEM(gradient.shape, BF16),
        dma((NMAT + 3,)),
        dma((4,)),
        dma((6,)),
        dma((3, 3)),
        dma((2, 3, 3)),
        dma((3,)),
        dma((3,)),
        dma((3,)),
        dma((3,)),
        dma((8,)),
        pltpu.SemaphoreType.REGULAR((3,)),
    ]
    held = [pltpu.with_memory_space_constraint(a, pltpu.HBM) for a in (gradient, basis, moment_m, moment_v)]
    made = pl.pallas_call(
        functools.partial(kernel, depth),
        out_shape=outs,
        in_specs=[anywhere] * 4,
        out_specs=(anywhere,) * 4,
        scratch_shapes=scratch,
        compiler_params=pltpu.CompilerParams(
            collective_id=0, has_side_effects=True, vmem_limit_bytes=40 * 1024 * 1024
        ),
        name="galore_step",
    )(*held)
    return pl.pallas_call(
        put,
        out_shape=outs,
        in_specs=[anywhere] * 4,
        out_specs=(pl.BlockSpec(memory_space=pltpu.HBM),) * 4,
        scratch_shapes=[dma((4,))],
        compiler_params=pltpu.CompilerParams(vmem_limit_bytes=16 * 1024 * 1024),
        name="put",
    )(*made)


def solution(mesh):
    placed = (
        P(None, ("tensor", "section"), "shard"),
        P(None, ("tensor", "section"), None),
        P(None, ("shard", "tensor", "section"), None),
        P(None, ("shard", "tensor", "section"), None),
    )
    return jax.shard_map(
        functools.partial(per_device, mesh.shape["shard"] // 2),
        mesh=mesh,
        in_specs=placed,
        out_specs=placed,
        check_vma=False,
    )
```

```python
import functools
import math

import jax
import jax.numpy as jnp
from jax import lax
from jax.experimental import pallas as pl
from jax.experimental.pallas import tpu as pltpu
from jax.sharding import PartitionSpec as P

D = 2048
NS_ITERS = 4
NMAT = 6
RANK = 256
ROWS = 128
RING = 4
PART = 32
SETS = ((0, 3), (1, 4), (2, 5))

beta_one = 0.9
beta_two = 0.999
bias_one = 1.0 - 0.9**10
bias_two = 1.0 - 0.999**10
eps_adam = 1e-08
galore_gain = 4.0

F32 = jnp.float32
BF16 = jnp.bfloat16
MESH = pl.DeviceIdType.MESH


def dot(a, b, ca, cb):
    return lax.dot_general(a, b, (((ca,), (cb,)), ((), ())), preferred_element_type=F32)


def split(a):
    high = a.astype(BF16)
    return high, (a - high.astype(F32)).astype(BF16)


def dot3(a, b, ca=1, cb=0):
    (ah, al), (bh, bl) = a, b
    return dot(ah, bh, ca, cb) + (dot(ah, bl, ca, cb) + dot(al, bh, ca, cb))


def plane(k):
    return k + k // 3


def kernel(
    depth,
    g_hbm,
    b_hbm,
    m_hbm,
    v_hbm,
    delta_out,
    basis_out,
    m_out,
    v_out,
    g_v,
    b_v,
    m_v,
    v_v,
    p_f,
    p_b,
    r1,
    rel1,
    q_f,
    q_b,
    r2,
    rough,
    step,
    t_own,
    t_in,
    u_b,
    d_in,
    s_f,
    gram,
    gram_in,
    gram_all,
    base,
    del_v,
    load_sem,
    store_sem,
    ring_send,
    rs_recv,
    ag_recv,
    t_recv,
    f_send,
    f_recv,
    fc_recv,
    one_sem,
    told,
):
    t_send, d_send, d_recv, gr_send, gr_recv, ga_send, ga_recv, fc_send = (one_sem.at[i] for i in range(8))
    shard = lax.axis_index("shard")
    x = lax.axis_index("tensor")
    y = lax.axis_index("section")
    z, core = shard // 2, lax.rem(shard, 2)
    partner = {"shard": z * 2 + (1 - core)}
    places = {"tensor": x, "section": y}
    matrix = z - z // 4
    owner = jnp.logical_and(lax.rem(z, 4) != 3, core == lax.rem(matrix, 2))

    def local(src, dst, sem):
        copy = pltpu.make_async_copy(src, dst, sem)
        copy.start()
        return copy

    def remote(src, dst, send_sem, recv_sem, where):
        return pltpu.make_async_remote_copy(
            src_ref=src,
            dst_ref=dst,
            send_sem=send_sem,
            recv_sem=recv_sem,
            device_id=where,
            device_id_type=MESH,
        )

    def arrived(like, sem):
        remote(like, like, sem, sem, partner).wait_recv()

    def departed(like, sem):
        remote(like, like, sem, sem, partner).wait_send()

    barrier = pltpu.get_barrier_semaphore()
    peers = [
        {"tensor": lax.rem(x + dx, RING), "section": lax.rem(y + dy, RING)}
        for dx in range(RING)
        for dy in range(RING)
        if (dx == 0) != (dy == 0) and 2 not in (dx, dy)
    ]
    beside = [{"shard": lax.rem(z + dz, depth) * 2 + core} for dz in (1, depth - 1)]
    peers += beside
    peers.append(partner)
    for there in peers:
        pl.semaphore_signal(barrier, inc=1, device_id=there, device_id_type=MESH)

    b_load = local(b_hbm, b_v, load_sem.at[NMAT])
    g_load = {k: local(g_hbm.at[k], g_v.at[k], load_sem.at[k]) for group in SETS for k in group}
    m_load = local(m_hbm, m_v, load_sem.at[NMAT + 1])
    v_load = local(v_hbm, v_v, load_sem.at[NMAT + 2])

    def project(k):
        g_load[k].wait()
        part = dot(g_v[k], b_v[k], 0, 0).reshape(RING, RING, PART, RANK)
        p_f[k] = part
        p_b[k] = part.astype(BF16)

    b_load.wait()
    for k in SETS[0]:
        project(k)
    pl.semaphore_wait(barrier, len(peers))

    def tell(turn):
        for there in beside:
            pl.semaphore_signal(told.at[turn], inc=1, device_id=there, device_id_type=MESH)

    def hear(turn):
        pl.semaphore_wait(told.at[turn], len(beside))
        if turn < 2:
            tell(turn + 1)

    tell(0)

    def ring_of(k, stage):
        name = ("tensor", "section")[(stage + (k >= 3)) % 2]
        at = places[name]
        plus, minus, far = (lax.rem(at + i, RING) for i in (1, 3, 2))
        return name, at, plus, minus, far

    def half(h, size):
        return pl.ds(h * size, size)

    def across(k, stage, landing, sem, sources):
        name, at, plus, minus, far = ring_of(k, stage)
        for slot, to in enumerate((far, plus, minus)):
            remote(sources(to), landing(slot), ring_send.at[sem[0]], sem[1], {name: to}).start()

    def piece(source, k, at, h):
        if k < 3:
            return source.at[k, at, half(h, 2)]
        return source.at[k, half(h, 2), at]

    def rs_push(k, src, slot, to):
        sem = rs_recv.at[k % 3, int(slot >= 2)]
        remote(src, r1.at[k, slot], ring_send.at[0], sem, {ring_of(k, 0)[0]: to}).start()

    def rs_begin(group):
        for k in group:
            if group != SETS[0]:
                project(k)
            name, at, plus, minus, far = ring_of(k, 0)
            rs_push(k, piece(p_b, k, far, 0), 0, plus)
            rs_push(k, piece(p_b, k, far, 1), 1, minus)

    def rs_direct(group):
        for k in group:
            name, at, plus, minus, far = ring_of(k, 0)
            rs_push(k, piece(p_b, k, plus, 1), 2, plus)
            rs_push(k, piece(p_b, k, minus, 0), 3, minus)

    def rs_relay(group):
        arrived(r1.at[0, pl.ds(0, 4)], rs_recv.at[group[0] % 3, 0])
        for k in group:
            name, at, plus, minus, far = ring_of(k, 0)
            for slot, to in ((0, plus), (1, minus)):
                own = piece(p_f, k, to, slot)[...]
                rel1[k, slot] = (own + r1[k, slot].astype(F32)).astype(BF16)
                rs_push(k, rel1.at[k, slot], slot + 4, to)

    def rs_turn(group):
        arrived(r1.at[pl.ds(0, 2), pl.ds(0, 4)], rs_recv.at[group[0] % 3, 1])
        for k in group:
            at = ring_of(k, 0)[1]
            for h, (one, two) in enumerate(((3, 4), (2, 5))):
                own = piece(p_f, k, at, h)[...]
                total = own + (r1[k, one].astype(F32) + r1[k, two].astype(F32))
                q_f[k, 2 * h : 2 * h + 2] = total
                q_b[k, 2 * h : 2 * h + 2] = total.astype(BF16)
            across(k, 1, lambda slot: r2.at[k, slot], (1, rs_recv.at[k % 3, 2]), lambda to: q_b.at[k, to])

    def ag_begin(held, kind, group):
        for k in group:
            own = held.at[k, x, y]
            across(k, 1, lambda slot: own, (2 + 2 * kind, ag_recv.at[kind, k % 3, 2]), lambda to: own)

    def ag_push(held, kind, k, at, h, slot, to):
        sem = ag_recv.at[kind, k % 3, int(slot not in (0, 3))]
        part = piece(held, k, at, h)
        remote(part, part, ring_send.at[3 + 2 * kind], sem, {ring_of(k, 0)[0]: to}).start()

    def ag_turn(held, kind, group):
        arrived(r2.at[pl.ds(0, 2)], ag_recv.at[kind, group[0] % 3, 2])
        for k in group:
            name, at, plus, minus, far = ring_of(k, 0)
            ag_push(held, kind, k, at, 0, 0, plus)
            ag_push(held, kind, k, at, 1, 3, minus)

    def ag_direct(held, kind, group):
        for k in group:
            name, at, plus, minus, far = ring_of(k, 0)
            ag_push(held, kind, k, at, 1, 1, plus)
            ag_push(held, kind, k, at, 0, 2, minus)

    def ag_relay(held, kind, group):
        arrived(r1.at[0, pl.ds(0, 4)], ag_recv.at[kind, group[0] % 3, 0])
        for k in group:
            name, at, plus, minus, far = ring_of(k, 0)
            ag_push(held, kind, k, minus, 0, 4, plus)
            ag_push(held, kind, k, plus, 1, 5, minus)

    def ag_full(held, kind, group):
        arrived(r2.at[pl.ds(0, 2)], ag_recv.at[kind, group[0] % 3, 2])
        for k in group:
            name, at, plus, minus, far = ring_of(k, 0)
            for to in (far, plus, minus):
                for h in range(2):
                    part = piece(held, k, at, h)
                    remote(part, part, ring_send.at[3 + 2 * kind], ag_recv.at[kind, k % 3, 1], {name: to}).start()

    def ag_whole(kind, group):
        arrived(r1.at[pl.ds(0, 2)], ag_recv.at[kind, group[0] % 3, 1])

    def ag_finish(kind, group):
        arrived(r1.at[pl.ds(0, 2), pl.ds(0, 4)], ag_recv.at[kind, group[0] % 3, 1])

    def core_copy(k):
        return remote(t_own.at[k], t_in.at[k], t_send, t_recv.at[k % 3], partner)

    def plane_copy(k):
        slot = lax.rem(z - plane(k) + depth, depth)
        return remote(u_b.at[k], d_in.at[slot], d_send, d_recv, {"shard": 2 * plane(k) + k % 2})

    def settle(group):
        arrived(r2.at[pl.ds(0, 2)], rs_recv.at[group[0] % 3, 2])
        lows = {}
        for k in group:
            own = q_f[k, ring_of(k, 1)[1]]
            total = own + (r2[k, 0].astype(F32) + r2[k, 1].astype(F32) + r2[k, 2].astype(F32))
            lows[k] = total * (1.0 / math.sqrt(D))
            rough[k, x, y] = lows[k].astype(BF16)
        ag_begin(rough, 0, group)
        if group == SETS[0]:
            m_load.wait()
            v_load.wait()
        for k in group:
            first = beta_one * m_v[k] + (1.0 - beta_one) * lows[k]
            second = beta_two * v_v[k] + (1.0 - beta_two) * lows[k] * lows[k]
            m_v[k] = first
            v_v[k] = second
            step[k, x, y] = (first / bias_one / (jnp.sqrt(second / bias_two) + eps_adam)).astype(BF16)

    def multiply(group):
        ag_whole(0, group)

        def product(k):
            t_own[k] = dot(g_v[k], rough[k].reshape(RING * RING * PART, RANK), 1, 0)

        for parity in range(2):
            kept, given = sorted(group, key=lambda k: k % 2 != parity)

            @pl.when(core == parity)
            def _():
                product(given)
                core_copy(given).start()
                product(kept)

    def scatter(group):
        for k in group:

            @pl.when(core == k % 2)
            def _():
                arrived(t_in.at[k], t_recv.at[k % 3])
                both = t_own[k] + t_in[k]

                @pl.when(z == plane(k))
                def _():
                    s_f[...] = both

                @pl.when(z != plane(k))
                def _():
                    u_b[k] = both.astype(BF16)
                    plane_copy(k).start()

    for task in (
        rs_begin,
        rs_direct,
        rs_relay,
        rs_turn,
        settle,
        functools.partial(ag_full, rough, 0),
        functools.partial(ag_begin, step, 1),
    ):
        for group in SETS:
            task(group)
        if task in (rs_relay, settle):
            hear(int(task is settle))
    hear(2)
    for group in SETS:
        multiply(group)
        scatter(group)
    for task in (functools.partial(ag_turn, step, 1), functools.partial(ag_direct, step, 1)):
        for group in SETS:
            task(group)

    stores = [local(m_v, m_out, store_sem.at[0]), local(v_v, v_out, store_sem.at[1])]
    chunk = RANK // (RING * RING)
    mine = pl.ds(pl.multiple_of((x * RING + y) * chunk, chunk), chunk)
    others = [(dx, dy) for dx in (2, 1, 3, 0) for dy in (2, 1, 3, 0) if dx or dy]

    @pl.when(owner)
    def _():
        arrived(d_in.at[pl.ds(1, depth - 1)], d_recv)
        total = s_f[...]
        for slot in range(1, depth):
            total = total + d_in[slot].astype(F32)
        s_f[...] = total
        whole = split(total)
        gram[...] = dot3(whole, whole, 0, 0)
        for dx, dy in others:
            tx, ty = lax.rem(x + dx, RING), lax.rem(y + dy, RING)
            theirs = pl.ds(pl.multiple_of((tx * RING + ty) * chunk, chunk), chunk)
            remote(
                gram.at[theirs], gram_in.at[dx * RING + dy], gr_send, gr_recv, {"tensor": tx, "section": ty}
            ).start()

    for group in SETS:
        ag_relay(step, 1, group)

    @pl.when(owner)
    def _():
        arrived(gram_in.at[pl.ds(1, RING * RING - 1)], gr_recv)
        total = gram[mine]
        for slot in range(1, RING * RING):
            total = total + gram_in[slot]
        gram_all[mine] = total
        for dx, dy in others:
            there = {"tensor": lax.rem(x + dx, RING), "section": lax.rem(y + dy, RING)}
            remote(gram_all.at[mine], gram_all.at[mine], ga_send, ga_recv, there).start()

    for group in SETS:
        ag_finish(1, group)
        for k in group:
            product = dot(b_v[k], step[k].reshape(RING * RING * PART, RANK), 1, 1)
            del_v[k] = (-galore_gain / math.sqrt(D) * product).astype(BF16)
    stores.append(local(del_v, delta_out, store_sem.at[2]))

    @pl.when(owner)
    def _():
        arrived(gram_in.at[pl.ds(1, RING * RING - 1)], ga_recv)
        gram0 = gram_all[...]
        row_sum = jnp.sum(jnp.abs(gram0), axis=1, keepdims=True)
        bound = jnp.max(row_sum, axis=0, keepdims=True) + 1e-06
        iterate = s_f[...] / jnp.sqrt(bound)
        gram_mat = gram0 / bound
        line = lax.broadcasted_iota(jnp.int32, (RANK, RANK), 0)
        column = lax.broadcasted_iota(jnp.int32, (RANK, RANK), 1)
        identity = jnp.where(line == column, 1.5, 0.0).astype(F32)
        for turn_index in range(NS_ITERS):
            factor = split(identity - 0.5 * gram_mat)
            if turn_index + 1 < NS_ITERS:
                gram_mat = dot3(split(dot3(split(gram_mat), factor)), factor)
            iterate = dot3(split(iterate), factor)
        base[...] = (math.sqrt(D) * iterate).astype(BF16)
        for dz in (3, 5, 2, 6, 1, 7):
            there = {"shard": lax.rem(z + dz, depth) * 2 + core}
            remote(base, basis_out.at[matrix], f_send.at[matrix // 2], f_recv.at[matrix // 2], there).start()
        remote(base, basis_out.at[matrix], fc_send, fc_recv.at[matrix // 2], partner).start()
        local(base, basis_out.at[matrix], store_sem.at[3])

    def pass_on(k, offset):
        for source, target, part in ((3, 4, 0), (5, 4, 1)):
            if source == offset:
                rows = pl.ds(0, ROWS) if part is None else half(part, ROWS // 2)
                there = {"shard": lax.rem(z + (target - source) + depth, depth) * 2 + core}
                held = basis_out.at[k, rows]
                remote(held, held, f_send.at[k // 2], f_recv.at[k // 2], there).start()

    ordered = [k for group in SETS for k in group]
    for k in ordered:
        offset = lax.rem(z - plane(k) + depth, depth)

        @pl.when(jnp.logical_and(core == k % 2, offset != 0))
        def _():
            arrived(basis_out.at[k], f_recv.at[k // 2])
            for source in (3, 5):

                @pl.when(offset == source)
                def _():
                    pass_on(k, source)

            remote(basis_out.at[k], basis_out.at[k], fc_send, fc_recv.at[k // 2], partner).start()

    for k in ordered:

        @pl.when(core != k % 2)
        def _():
            arrived(basis_out.at[k], fc_recv.at[k // 2])

    for index, like in enumerate((r1, r2, r2, r1, r2, r1)):
        departed(like, ring_send.at[index])
    departed(t_own.at[pl.ds(0, 3)], t_send)

    @pl.when(owner)
    def _():
        departed(u_b.at[pl.ds(0, 2)], d_send)
        departed(gram_in.at[pl.ds(1, RING * RING - 1)], gr_send)
        departed(gram_in.at[pl.ds(1, RING * RING - 1)], ga_send)
        departed(d_in.at[pl.ds(0, 6)], f_send.at[matrix // 2])
        pltpu.make_async_copy(base, basis_out.at[matrix], store_sem.at[3]).wait()

    @pl.when(jnp.logical_not(owner))
    def _():
        departed(u_b.at[pl.ds(0, 3)], d_send)

    for k in range(NMAT):
        offset = lax.rem(z - plane(k) + depth, depth)

        @pl.when(jnp.logical_and(core == k % 2, jnp.logical_or(offset == 3, offset == 5)))
        def _():
            departed(r2.at[0:1, pl.ds(0, 2)], f_send.at[k // 2])

    departed(u_b.at[pl.ds(0, 3)], fc_send)
    for copy in stores:
        copy.wait()


def put(*refs):
    sources, targets, sem = refs[:4], refs[4:8], refs[8]
    copies = [pltpu.make_async_copy(a, b, sem.at[i]) for i, (a, b) in enumerate(zip(sources, targets))]
    for copy in copies:
        copy.start()
    for copy in copies:
        copy.wait()


def per_device(depth, gradient, basis, moment_m, moment_v):
    dma = pltpu.SemaphoreType.DMA
    anywhere = pl.BlockSpec(memory_space=pl.ANY)
    shape = jax.ShapeDtypeStruct
    outs = (
        shape(gradient.shape, BF16),
        shape(basis.shape, BF16),
        shape(moment_m.shape, F32),
        shape(moment_v.shape, F32),
    )
    scratch = [
        pltpu.VMEM(gradient.shape, BF16),
        pltpu.VMEM(basis.shape, BF16),
        pltpu.VMEM(moment_m.shape, F32),
        pltpu.VMEM(moment_v.shape, F32),
        pltpu.VMEM((NMAT, RING, RING, PART, RANK), F32),
        pltpu.VMEM((NMAT, RING, RING, PART, RANK), BF16),
        pltpu.VMEM((NMAT, 6, 2, PART, RANK), BF16),
        pltpu.VMEM((NMAT, 2, 2, PART, RANK), BF16),
        pltpu.VMEM((NMAT, RING, PART, RANK), F32),
        pltpu.VMEM((NMAT, RING, PART, RANK), BF16),
        pltpu.VMEM((NMAT, 3, PART, RANK), BF16),
        pltpu.VMEM((NMAT, RING, RING, PART, RANK), BF16),
        pltpu.VMEM((NMAT, RING, RING, PART, RANK), BF16),
        pltpu.VMEM((NMAT, ROWS, RANK), F32),
        pltpu.VMEM((NMAT, ROWS, RANK), F32),
        pltpu.VMEM((NMAT, ROWS, RANK), BF16),
        pltpu.VMEM((depth, ROWS, RANK), BF16),
        pltpu.VMEM((ROWS, RANK), F32),
        pltpu.VMEM((RANK, RANK), F32),
        pltpu.VMEM((RING * RING, RANK // (RING * RING), RANK), F32),
        pltpu.VMEM((RANK, RANK), F32),
        pltpu.VMEM((ROWS, RANK), BF16),
        pltpu.VMEM(gradient.shape, BF16),
        dma((NMAT + 3,)),
        dma((4,)),
        dma((6,)),
        dma((3, 3)),
        dma((2, 3, 3)),
        dma((3,)),
        dma((3,)),
        dma((3,)),
        dma((3,)),
        dma((8,)),
        pltpu.SemaphoreType.REGULAR((3,)),
    ]
    held = [pltpu.with_memory_space_constraint(a, pltpu.HBM) for a in (gradient, basis, moment_m, moment_v)]
    made = pl.pallas_call(
        functools.partial(kernel, depth),
        out_shape=outs,
        in_specs=[anywhere] * 4,
        out_specs=(anywhere,) * 4,
        scratch_shapes=scratch,
        compiler_params=pltpu.CompilerParams(
            collective_id=0, has_side_effects=True, vmem_limit_bytes=40 * 1024 * 1024
        ),
        name="galore_step",
    )(*held)
    return pl.pallas_call(
        put,
        out_shape=outs,
        in_specs=[anywhere] * 4,
        out_specs=(pl.BlockSpec(memory_space=pltpu.HBM),) * 4,
        scratch_shapes=[dma((4,))],
        compiler_params=pltpu.CompilerParams(vmem_limit_bytes=16 * 1024 * 1024),
        name="put",
    )(*made)


def solution(mesh):
    placed = (
        P(None, ("tensor", "section"), "shard"),
        P(None, ("tensor", "section"), None),
        P(None, ("shard", "tensor", "section"), None),
        P(None, ("shard", "tensor", "section"), None),
    )
    return jax.shard_map(
        functools.partial(per_device, mesh.shape["shard"] // 2),
        mesh=mesh,
        in_specs=placed,
        out_specs=placed,
        check_vma=False,
    )
```
